32 devices in a mesh: seq: 4 (over y, x), dp: 8 (over z, core).
Axes of the slice: x: 2, y: 2, z: 4, core: 2. Of those that a mesh axis runs over, the one named last changes fastest.
Arguments:
- layer_input: bfloat16 [8, 1024, 8192], P('dp', 'seq'), may hold values from -400 to 400
- frozen_queries: bfloat16 [8, 1024, 6144], P('dp', 'seq'), may hold values from -70 to 70
- frozen_keys: bfloat16 [8, 1024, 768], P('dp', 'seq'), may hold values from -6 to 6
- frozen_values: bfloat16 [8, 1024, 768], P('dp', 'seq'), may hold values from -6 to 6
- output_gradient: bfloat16 [8, 1024, 6144], P('dp', 'seq'), may hold values from -6 to 6
- norm_scale_vector: bfloat16 [8192], replicated, may hold values from 0.5 to 1.5
- query_down_weight: bfloat16 [8, 8192], replicated, may hold values from -0.0625 to 0.0625
- query_up_weight: bfloat16 [8, 6144], replicated, may hold values from -2 to 2
- value_down_weight: bfloat16 [8, 8192], replicated, may hold values from -0.0625 to 0.0625
- value_up_weight: bfloat16 [8, 768], replicated, may hold values from -2 to 2
- head_ordering: int32 [6], replicated, may hold values from 0 to 5, each once
Outputs:
- grad_query_a: float32 [8, 8192], replicated
- grad_query_b: float32 [8, 6144], replicated
- grad_value_a: float32 [8, 8192], replicated
- grad_value_b: float32 [8, 768], replicated
- grad_gain: float32 [8192], replicated
The draws below stay inside these ranges and needn't reach their ends.
Inputs may be any that keep to these rules, and one draw needn't show every extreme that they name: `head_ordering`: a permutation of the 6 key-value heads.
All inputs are finite; a program needn't handle non-finite values.
Results may differ from the reference program's by a relative error of at most 0.012.
The reference program's roundings to bfloat16 on the way count: a program that leaves them out, or rounds other values in their place, can miss the bound.
Values may be sent and summed in bfloat16 or wider, within the bound.
A program may use at most 128 MiB of HBM per device.

```python
import math
from functools import partial
import jax
import jax.numpy as jnp
from jax import lax

MODEL_WIDTH = 8192
HEAD_SIZE = 128
QUERY_HEADS = 48
KEY_VALUE_HEADS = 6
ADAPTER_RANK = 8
G = 512
SEQUENCE_LENGTH = 1024
BATCH_COUNT = 8


def drawn_pair(key):
    query_layout = (BATCH_COUNT, SEQUENCE_LENGTH, KEY_VALUE_HEADS, QUERY_HEADS // KEY_VALUE_HEADS, HEAD_SIZE)
    key_layout = (BATCH_COUNT, SEQUENCE_LENGTH, KEY_VALUE_HEADS, HEAD_SIZE)
    key_rows = jax.random.truncated_normal(jax.random.fold_in(key, 102), -6.0, 6.0, key_layout, jnp.float32)
    queries = jax.random.truncated_normal(jax.random.fold_in(key, 103), -6.0, 6.0, query_layout, jnp.float32)
    return (queries, key_rows)


def draw_frozen_queries(key, part):
    queries, key_rows = drawn_pair(key)
    return queries.reshape(BATCH_COUNT, SEQUENCE_LENGTH, QUERY_HEADS * HEAD_SIZE).astype(jnp.bfloat16)


def draw_frozen_keys(key, part):
    queries, key_rows = drawn_pair(key)
    return key_rows.reshape(BATCH_COUNT, SEQUENCE_LENGTH, KEY_VALUE_HEADS * HEAD_SIZE).astype(jnp.bfloat16)


def draw_layer_input(key, part):
    row_scale = jnp.exp(jax.random.uniform(jax.random.fold_in(key, 201), (BATCH_COUNT, SEQUENCE_LENGTH, 1), jnp.float32, 0.0, math.log(10.0)))
    col_scale = jnp.exp(jax.random.uniform(jax.random.fold_in(key, 202), (1, 1, MODEL_WIDTH), jnp.float32, 0.0, math.log(10.0)))
    base = jax.random.truncated_normal(jax.random.fold_in(key, 203), -4.0, 4.0, (BATCH_COUNT, SEQUENCE_LENGTH, MODEL_WIDTH), jnp.float32)
    return (base * row_scale * col_scale).astype(jnp.bfloat16)


def block_scale(key, shape, shards, low, high):
    factor_of = 1.0
    for dim, shards_of in shards:
        heights = jax.random.uniform(jax.random.fold_in(jax.random.fold_in(key, 6), dim), (shards_of,), jnp.float32, low / len(shards), high / len(shards))
        factor_of = factor_of * jnp.repeat(jnp.exp(heights), shape[dim] // shards_of).reshape((-1,) + (1,) * (len(shape) - 1 - dim))
    return factor_of


def normal_values(stream_key, shape, deviation, reach, cuts=(), kind=jnp.bfloat16):
    loudness = block_scale(stream_key, shape, cuts, -0.22, 0.18) if cuts else 1.0
    values = jax.random.normal(stream_key, shape, jnp.float32) * deviation * loudness
    return jnp.minimum(jnp.maximum(values, -reach), reach).astype(kind)


def setup_inputs(seed: int = 0) -> dict:
    arg_keys = jax.random.split(jax.random.key(seed), 12)
    layer_input = draw_layer_input(jax.random.fold_in(arg_keys[11], 71), 0)
    frozen_queries = draw_frozen_queries(jax.random.fold_in(arg_keys[11], 71), 0)
    frozen_keys = draw_frozen_keys(jax.random.fold_in(arg_keys[11], 71), 0)
    frozen_values = normal_values(arg_keys[3], (BATCH_COUNT, SEQUENCE_LENGTH, KEY_VALUE_HEADS * HEAD_SIZE), 1.0, 6.0, ((0, 8), (1, 4)))
    output_gradient = normal_values(arg_keys[4], (BATCH_COUNT, SEQUENCE_LENGTH, QUERY_HEADS * HEAD_SIZE), 1.0, 6.0, ((0, 8), (1, 4)))
    norm_scale_vector = jnp.clip(jax.random.uniform(arg_keys[5], (MODEL_WIDTH,), jnp.float32, 0.5, 1.5), 0.5, 1.5).astype(jnp.bfloat16)
    query_down_weight = normal_values(arg_keys[6], (ADAPTER_RANK, MODEL_WIDTH), MODEL_WIDTH ** -0.5, 0.0625)
    query_up_weight = normal_values(arg_keys[7], (ADAPTER_RANK, QUERY_HEADS * HEAD_SIZE), ADAPTER_RANK ** -0.5, 2.0)
    value_down_weight = normal_values(arg_keys[8], (ADAPTER_RANK, MODEL_WIDTH), MODEL_WIDTH ** -0.5, 0.0625)
    value_up_weight = normal_values(arg_keys[9], (ADAPTER_RANK, KEY_VALUE_HEADS * HEAD_SIZE), ADAPTER_RANK ** -0.5, 2.0)
    head_ordering = jax.random.permutation(arg_keys[10], KEY_VALUE_HEADS).astype(jnp.int32)
    return dict(layer_input=layer_input, frozen_queries=frozen_queries, frozen_keys=frozen_keys, frozen_values=frozen_values, output_gradient=output_gradient, norm_scale_vector=norm_scale_vector, query_down_weight=query_down_weight, query_up_weight=query_up_weight, value_down_weight=value_down_weight, value_up_weight=value_up_weight, head_ordering=head_ordering)


EPS = 1e-05
ADAPTER_SCALE = 2.0

def attend_group(query_rows, key_rows, values, grad_out, allowed):
    factor = 1.0 / math.sqrt(HEAD_SIZE)
    keys_f = key_rows.astype(jnp.float32)
    values_f = values.astype(jnp.float32)
    grads_f = grad_out.astype(jnp.float32)
    scores = jnp.einsum('tgd,ud->gtu', query_rows.astype(jnp.float32), keys_f) * factor
    scores = jnp.where(allowed[None], scores, -jnp.inf)
    row_max = lax.optimization_barrier(jnp.max(scores, axis=-1, keepdims=True))
    exponent = jnp.exp(scores - row_max)
    probs_full = exponent / lax.optimization_barrier(jnp.sum(exponent, axis=-1, keepdims=True))
    weights = lax.optimization_barrier(probs_full.astype(jnp.bfloat16)).astype(jnp.float32)
    attended = jnp.einsum('gtu,ud->tgd', weights, values_f)
    delta = lax.optimization_barrier(jnp.sum(grads_f * attended, axis=-1))
    dprob = jnp.einsum('tgd,ud->gtu', grads_f, values_f)
    dscore = probs_full * (dprob - delta.T[:, :, None])
    dscore_b = lax.optimization_barrier(dscore.astype(jnp.bfloat16)).astype(jnp.float32)
    query_gradient = jnp.einsum('gtu,ud->tgd', dscore_b, keys_f) * factor
    value_gradient = jnp.einsum('gtu,tgd->ud', weights, grads_f)
    return (query_gradient, value_gradient)

def head_grads(operands):
    query_h, keys_h, values_h, grads_h, offset = operands

    def regroup(array):
        rolled_array = jnp.roll(array, -offset, axis=0)
        return rolled_array.reshape((SEQUENCE_LENGTH // G, G) + array.shape[1:])
    positions = jnp.arange(G)
    causal = positions[None, :] <= positions[:, None]
    query_gradient, value_gradient = jax.vmap(partial(attend_group, allowed=causal))(regroup(query_h), regroup(keys_h), regroup(values_h), regroup(grads_h))
    query_gradient = jnp.roll(query_gradient.reshape(query_h.shape), offset, axis=0)
    value_gradient = jnp.roll(value_gradient.reshape(keys_h.shape), offset, axis=0)
    return (query_gradient.astype(jnp.bfloat16), value_gradient.astype(jnp.bfloat16))

def reference(layer_input, frozen_queries, frozen_keys, frozen_values, output_gradient, norm_scale_vector, query_down_weight, query_up_weight, value_down_weight, value_up_weight, head_ordering):
    displaced_index = head_ordering[:KEY_VALUE_HEADS // 2]
    displaced_mask = jnp.any(displaced_index[:, None] == jnp.arange(KEY_VALUE_HEADS, dtype=jnp.int32)[None, :], axis=0)
    shift_amounts = jnp.where(displaced_mask, G // 2, 0).astype(jnp.int32)

    def one_sequence(totals, operands):
        hidden_s, query_slices, key_slices, value_slices, gradient_slices = operands
        hidden_f = hidden_s.astype(jnp.float32)
        inverse = lax.rsqrt(lax.optimization_barrier(jnp.mean(hidden_f * hidden_f, axis=-1, keepdims=True)) + EPS)
        unit = hidden_f * inverse
        normalized_input = (unit * norm_scale_vector.astype(jnp.float32)).astype(jnp.bfloat16)
        query_inner = jnp.dot(normalized_input, query_down_weight.T, preferred_element_type=jnp.float32).astype(jnp.bfloat16)
        value_inner = jnp.dot(normalized_input, value_down_weight.T, preferred_element_type=jnp.float32).astype(jnp.bfloat16)
        query_rows = (query_slices.astype(jnp.float32) + ADAPTER_SCALE * jnp.dot(query_inner, query_up_weight, preferred_element_type=jnp.float32)).astype(jnp.bfloat16)
        value_rows = (value_slices.astype(jnp.float32) + ADAPTER_SCALE * jnp.dot(value_inner, value_up_weight, preferred_element_type=jnp.float32)).astype(jnp.bfloat16)
        head_wise = (jnp.moveaxis(query_rows.reshape(SEQUENCE_LENGTH, KEY_VALUE_HEADS, QUERY_HEADS // KEY_VALUE_HEADS, HEAD_SIZE), 1, 0), jnp.moveaxis(key_slices.reshape(SEQUENCE_LENGTH, KEY_VALUE_HEADS, HEAD_SIZE), 1, 0), jnp.moveaxis(value_rows.reshape(SEQUENCE_LENGTH, KEY_VALUE_HEADS, HEAD_SIZE), 1, 0), jnp.moveaxis(gradient_slices.reshape(SEQUENCE_LENGTH, KEY_VALUE_HEADS, QUERY_HEADS // KEY_VALUE_HEADS, HEAD_SIZE), 1, 0), shift_amounts)
        query_gradient, value_gradient = lax.map(head_grads, head_wise)
        query_gradient = jnp.moveaxis(query_gradient, 0, 1).reshape(SEQUENCE_LENGTH, QUERY_HEADS * HEAD_SIZE)
        value_gradient = jnp.moveaxis(value_gradient, 0, 1).reshape(SEQUENCE_LENGTH, KEY_VALUE_HEADS * HEAD_SIZE)
        query_up_unscaled = ADAPTER_SCALE * jnp.dot(query_inner.T, query_gradient, preferred_element_type=jnp.float32)
        value_up_unscaled = ADAPTER_SCALE * jnp.dot(value_inner.T, value_gradient, preferred_element_type=jnp.float32)
        query_gradient_inner = (ADAPTER_SCALE * jnp.dot(query_gradient, query_up_weight.T, preferred_element_type=jnp.float32)).astype(jnp.bfloat16)
        value_gradient_inner = (ADAPTER_SCALE * jnp.dot(value_gradient, value_up_weight.T, preferred_element_type=jnp.float32)).astype(jnp.bfloat16)
        raw_qa = jnp.dot(query_gradient_inner.T, normalized_input, preferred_element_type=jnp.float32)
        raw_va = jnp.dot(value_gradient_inner.T, normalized_input, preferred_element_type=jnp.float32)
        normalized_gradient = jnp.dot(query_gradient_inner, query_down_weight, preferred_element_type=jnp.float32) + jnp.dot(value_gradient_inner, value_down_weight, preferred_element_type=jnp.float32)
        raw_gain = lax.optimization_barrier(jnp.sum(normalized_gradient * unit, axis=0))
        fresh = (raw_qa, query_up_unscaled, raw_va, value_up_unscaled, raw_gain)
        return (tuple((total + term for total, term in zip(totals, fresh))), None)
    start_position = (jnp.zeros((ADAPTER_RANK, MODEL_WIDTH), jnp.float32), jnp.zeros((ADAPTER_RANK, QUERY_HEADS * HEAD_SIZE), jnp.float32), jnp.zeros((ADAPTER_RANK, MODEL_WIDTH), jnp.float32), jnp.zeros((ADAPTER_RANK, KEY_VALUE_HEADS * HEAD_SIZE), jnp.float32), jnp.zeros((MODEL_WIDTH,), jnp.float32))
    totals, unused = lax.scan(one_sequence, start_position, (layer_input, frozen_queries, frozen_keys, frozen_values, output_gradient))
    squares = jnp.zeros((), jnp.float32)
    for part in totals:
        squares = squares + jnp.sum(part * part)
    listed_items = ADAPTER_RANK * (2 * MODEL_WIDTH + QUERY_HEADS * HEAD_SIZE + KEY_VALUE_HEADS * HEAD_SIZE) + MODEL_WIDTH
    factor = jnp.minimum(1.0, math.sqrt(listed_items) / jnp.sqrt(squares))
    return (totals[0] * factor, totals[1] * factor, totals[2] * factor, totals[3] * factor, totals[4] * factor)
```

```python
import functools
import math

import jax
import jax.numpy as jnp
from jax import lax
from jax.experimental import pallas as pl
from jax.experimental.pallas import tpu as pltpu
from jax.sharding import PartitionSpec as P

HEAD_SIZE = 128
CORES = 2
LANES = 128
TOGETHER = 2
CHUNKS = 4

EPS = 1e-05
ADAPTER_SCALE = 2.0
F32 = jnp.float32
BF16 = jnp.bfloat16
NT = (((1,), (1,)), ((), ()))
NN = (((1,), (0,)), ((), ()))
MESH = pl.DeviceIdType.MESH


def dot(left, right, dims):
    return lax.dot_general(left, right, dims, preferred_element_type=F32)


def stack(pieces):
    return jnp.concatenate(pieces, axis=0)


def beside(pieces):
    return jnp.concatenate(pieces, axis=1)


def split(value):
    high = value.astype(BF16)
    return high, (value - high.astype(F32)).astype(BF16)


def fused_kernel(
    seqs,
    planes,
    heads_ref,
    x_hbm,
    fq_hbm,
    grad_hbm,
    key_hbm,
    fv_hbm,
    scale_hbm,
    qdown_hbm,
    vdown_hbm,
    qup_hbm,
    vup_hbm,
    full_e,
    full_q,
    full_v,
    x,
    fq,
    grad,
    key,
    fv,
    scale,
    qdown,
    vdown,
    qup,
    vup,
    value,
    key_out,
    value_out,
    mid_out,
    key_in,
    value_in,
    mid_in,
    hand_out,
    hand_in,
    part_e,
    part_q,
    part_v,
    parts_e,
    parts_q,
    parts_v,
    column_e,
    column_q,
    column_v,
    sem_load,
    sem_pass_send,
    sem_pass_recv,
    sem_send,
    sem_recv,
    query_mid,
    query_mid_t,
    total_q,
    total_v,
    dvalue,
    keys_t,
    tiles,
):
    rows, width = x.shape
    rank = qdown.shape[0]
    kv, _, wide = fq.shape
    half = kv // 2
    per = wide // HEAD_SIZE
    queries = kv * wide
    factor = 1.0 / math.sqrt(HEAD_SIZE)
    group = seqs * CORES
    seq = lax.axis_index("seq")
    place = lax.axis_index("dp")
    plane = place // CORES
    me = seq * CORES + place % CORES
    parity = lax.rem(seq, 2)
    following = {"seq": lax.rem(seq + 1, seqs)}
    previous = {"seq": lax.rem(seq + seqs - 1, seqs)}

    def in_group(k):
        peer = lax.rem(me + k, group)
        return peer, {"seq": peer // CORES, "dp": plane * CORES + peer % CORES}

    def in_column(k):
        return {"dp": lax.rem(plane + k, planes) * CORES + place % CORES}

    loads = []

    def load(source, target):
        copy = pltpu.make_async_copy(source, target, sem_load.at[len(loads)])
        copy.start()
        loads.append(copy)
        return copy

    def by_head(source, target):
        size = target.shape[2]
        return [load(source.at[:, h * size : (h + 1) * size], target.at[h]) for h in range(kv)]

    block = width // CHUNKS
    get_key = by_head(key_hbm, key)
    get_small = [
        load(s, t) for s, t in ((scale_hbm, scale), (qdown_hbm, qdown), (vdown_hbm, vdown))
    ]
    get_x = [
        load(x_hbm.at[:, c * block : (c + 1) * block], x.at[:, c * block : (c + 1) * block])
        for c in range(CHUNKS)
    ]
    get_value = by_head(fv_hbm, fv) + by_head(vup_hbm, vup) + by_head(qup_hbm, qup)
    get_wide = by_head(fq_hbm, fq) + by_head(grad_hbm, grad)

    barrier = pltpu.get_barrier_semaphore()
    for k in range(1, group):
        pl.semaphore_signal(barrier, inc=1, device_id=in_group(k)[1], device_id_type=MESH)
    for k in range(1, planes):
        pl.semaphore_signal(barrier, inc=1, device_id=in_column(k), device_id_type=MESH)

    def remote(source, target, send, recv, device):
        copy = pltpu.make_async_remote_copy(
            src_ref=source,
            dst_ref=target,
            send_sem=send,
            recv_sem=recv,
            device_id=device,
            device_id_type=MESH,
        )
        copy.start()
        return copy

    passed = []

    def hand(source, target, device):
        i = len(passed)
        copy = remote(source, target, sem_pass_send.at[i], sem_pass_recv.at[i], device)
        passed.append(copy)
        return copy

    own_at = lambda i: (1 - parity) * half + i
    prior_at = lambda i: parity * half + i

    for copy in get_key:
        copy.wait()
    for i in range(half):
        key_out[i] = key[heads_ref[own_at(i)]]
    for copy in get_small:
        copy.wait()
    folded = []
    for i in range(width // LANES):
        cols = slice(i * LANES, (i + 1) * LANES)
        down = stack([qdown[:, cols].astype(F32), vdown[:, cols].astype(F32)])
        folded.append(stack(split(down * scale[i : i + 1, :].astype(F32))))

    squares = jnp.zeros((rows, LANES), F32)
    mids = jnp.zeros((rows, 4 * rank), F32)
    for c in range(CHUNKS):
        get_x[c].wait()
        each = block // LANES
        piece = x[:, c * block : (c + 1) * block]
        for b in range(each):
            part = piece[:, b * LANES : (b + 1) * LANES].astype(F32)
            squares = squares + part * part
        folds = beside(folded[c * each : (c + 1) * each])
        mids = mids + stack(
            [dot(piece[r * rows // 2 : (r + 1) * rows // 2], folds, NT) for r in range(2)]
        )
        if c == 0:
            pl.semaphore_wait(barrier, group + planes - 2)
            pass_key = [hand(key_out.at[i], key_in.at[i], following) for i in range(half)]
    inverse = lax.rsqrt(jnp.sum(squares, axis=1, keepdims=True) * (1.0 / width) + EPS)
    inverse_row = jnp.broadcast_to(inverse, (rows, LANES)).T[:rank]
    mids = ((mids[:, : 2 * rank] + mids[:, 2 * rank :]) * inverse).astype(BF16)
    twice = (mids * ADAPTER_SCALE).astype(BF16)
    query_mid[...] = twice[:, :rank]
    value_mid = twice[:, rank:]
    eye_r = lax.broadcasted_iota(jnp.int32, (2 * rank, 2 * rank), 0)
    eye_c = lax.broadcasted_iota(jnp.int32, (2 * rank, 2 * rank), 1)
    eye = jnp.where(eye_r == eye_c, ADAPTER_SCALE, 0.0).astype(BF16)
    mids_t = dot(eye, mids, NT)
    query_mid_t[...] = mids_t[:rank].astype(BF16)
    mid_out[...] = mids_t[rank:].astype(BF16)
    for copy in get_value:
        copy.wait()
    for h in range(kv):
        value[h] = (fv[h].astype(F32) + dot(value_mid, vup[h], NN)).astype(BF16)
    for i in range(half):
        value_out[i] = value[heads_ref[own_at(i)]]
    pass_mid = hand(mid_out, mid_in, following)
    pass_value = [hand(value_out.at[i], value_in.at[i], following) for i in range(half)]
    for copy in get_wide:
        copy.wait()

    together = TOGETHER
    groups = per // together
    part_rows = rows // 2
    span = together * part_rows
    log2e = factor * math.log2(math.e)
    scores_at, dprob_at, weights_at, dscore_at = tiles
    total_q[...] = jnp.zeros_like(total_q)
    total_v[...] = jnp.zeros_like(total_v)
    hand_out[...] = jnp.zeros_like(hand_out)
    used = queries + kv * HEAD_SIZE
    if used < part_e.shape[1]:
        part_e[:, used:] = jnp.zeros((rank, part_e.shape[1] - used), BF16)

    def piled(array):
        return stack([array[:, k * HEAD_SIZE : (k + 1) * HEAD_SIZE] for k in range(together)])

    def phase(with_prior):
        before = rows if with_prior else 0
        reaches = [before + part_rows, before + rows]
        place_of = prior_at if with_prior else own_at

        def both(i, head, mine, given):
            return stack([given[i], mine[head]]) if with_prior else mine[head]

        def opened(i, p):
            slot = p % 2
            head = heads_ref[place_of(i)]
            cols = slice(p * together * HEAD_SIZE, (p + 1) * together * HEAD_SIZE)
            keys = both(i, head, key, key_in)
            values = both(i, head, value, value_in)
            for a in range(2):
                at = slice(a * part_rows, (a + 1) * part_rows)
                reach = reaches[a]
                adapted = dot(query_mid[at, :], qup[head, :, cols], NN)
                query = (fq[head, at, cols].astype(F32) + adapted).astype(BF16)
                scores_at[slot][a][:reach, :] = dot(keys[:reach], piled(query), NT)
                dprob_at[slot][a][:reach, :] = dot(values[:reach], piled(grad[head, at, cols]), NT)

        def weighed(p):
            slot = p % 2
            key_pos = lax.broadcasted_iota(jnp.int32, (part_rows, span), 0)
            query_pos = lax.broadcasted_iota(jnp.int32, (part_rows, span), 1)
            causal = key_pos <= lax.rem(query_pos, part_rows)
            for a in range(2):
                reach = reaches[a]
                free = reach - part_rows
                scores = scores_at[slot][a][:reach, :]
                dprob = dprob_at[slot][a][:reach, :]
                diagonal = jnp.where(causal, scores[free:], -jnp.inf)
                scores = stack([scores[:free], diagonal]) if free else diagonal
                top = jnp.max(scores, axis=0, keepdims=True)
                exponent = jnp.exp2((scores - top) * log2e)
                probs = exponent * (1.0 / jnp.sum(exponent, axis=0, keepdims=True))
                weights = probs.astype(BF16)
                weights_at[slot][a][:reach, :] = weights
                delta = jnp.sum(weights.astype(F32) * dprob, axis=0, keepdims=True)
                dscore_at[slot][a][:reach, :] = (probs * (dprob - delta)).astype(BF16)

        def closed(i, p):
            slot = p % 2
            pos = place_of(i)
            head = heads_ref[pos]
            cols = slice(p * together * HEAD_SIZE, (p + 1) * together * HEAD_SIZE)
            terms, dqs = [], []
            for a in range(2):
                at = slice(a * part_rows, (a + 1) * part_rows)
                reach = reaches[a]
                grads = piled(grad[head, at, cols])
                terms.append(dot(weights_at[slot][a][:reach, :], grads, NN))
                dqs.append(dot(keys_t[:, :reach], dscore_at[slot][a][:reach, :], NN).astype(BF16))
            dv = stack([terms[1][: reaches[0]] + terms[0], terms[1][reaches[0] :]])
            if p:
                dv = dv + dvalue[: reaches[1], :]
            dquery = stack(
                [
                    beside([dq[:, k * part_rows : (k + 1) * part_rows] for dq in dqs])
                    for k in range(together)
                ]
            )
            at = pl.multiple_of(pos * wide + p * together * HEAD_SIZE, HEAD_SIZE)
            part_e[:, pl.ds(at, together * HEAD_SIZE)] = (
                dot(query_mid_t[...], dquery, NT) * factor
            ).astype(BF16)
            total_q[...] += dot(qup[head, :, cols], dquery, NN)
            if p < groups - 1:
                dvalue[: reaches[1], :] = dv
                return
            up = vup[head]
            mine = dv[before:].astype(BF16)
            raw = dot(mid_out[...], mine, NN)
            total_v[...] += dot(up, mine, NT)
            if before:
                others = dv[:before].astype(BF16)
                raw = raw + dot(mid_in[...], others, NN)
                hand_out[...] += dot(up, others, NT)
            at = pl.multiple_of(queries + pos * HEAD_SIZE, HEAD_SIZE)
            part_e[:, pl.ds(at, HEAD_SIZE)] = raw.astype(BF16)

        def arrived(i):
            for source, target, first in ((key_out, key_in, 0), (value_out, value_in, half + 1)):
                pltpu.make_async_remote_copy(
                    src_ref=source.at[i],
                    dst_ref=target.at[i],
                    send_sem=sem_pass_send.at[first + i],
                    recv_sem=sem_pass_recv.at[first + i],
                    device_id=following,
                    device_id_type=MESH,
                ).wait_recv()

        def transposed(i):
            keys_t[:, : reaches[1]] = both(i, heads_ref[place_of(i)], key, key_in).T

        if with_prior:
            pass_mid.wait_recv()
            arrived(0)
        last = (groups - 1) % 2
        for a in range(2):
            weights_at[last][a][...] = jnp.zeros_like(weights_at[last][a])
            dscore_at[last][a][...] = jnp.zeros_like(dscore_at[last][a])
        dvalue[...] = jnp.zeros_like(dvalue)
        transposed(0)
        opened(0, 0)

        def body(i, carry):
            later = lax.rem(i + 1, half)
            if with_prior:

                @pl.when(i < half - 1)
                def _():
                    arrived(i + 1)

            for p in range(groups):
                if p + 1 < groups:
                    opened(i, p + 1)
                else:
                    opened(later, 0)
                weighed(p)
                if p:
                    closed(i, p - 1)
                else:
                    closed(lax.rem(i + half - 1, half), groups - 1)
                    transposed(i)
            return carry

        lax.fori_loop(0, half, body, 0)
        closed(half - 1, groups - 1)

    phase(False)
    phase(True)
    pass_hand = hand(hand_out, hand_in, previous)

    sums = {
        "e": (part_e, parts_e, column_e, full_e, 0),
        "q": (part_q, parts_q, column_q, full_q, 1),
        "v": (part_v, parts_v, column_v, full_v, 2),
    }
    steps = 2 * (group - 1) + planes - 1
    sent = {name: [[], [], []] for name in sums}

    def share(array, index):
        piece = array.shape[1] // group
        return array.at[:, pl.ds(pl.multiple_of(index * piece, piece), piece)]

    def scatter(name):
        source, parts, _, _, base = sums[name]
        for k in range(1, group):
            peer, device = in_group(k)
            at = base * steps + k - 1
            sent[name][0].append(
                remote(
                    share(source, peer), parts.at[k - 1], sem_send.at[at], sem_recv.at[at], device
                )
            )

    def across(name):
        source, parts, column, _, base = sums[name]
        amount = share(source, me)[...].astype(F32)
        for k in range(1, group):
            sent[name][0][k - 1].wait_recv()
            amount = amount + parts[k - 1].astype(F32)
        column[plane] = amount.astype(BF16)
        for k in range(1, planes):
            at = base * steps + group - 1 + k - 1
            sent[name][1].append(
                remote(
                    column.at[plane],
                    column.at[plane],
                    sem_send.at[at],
                    sem_recv.at[at],
                    in_column(k),
                )
            )

    def gather(name):
        _, _, column, full, base = sums[name]
        for copy in sent[name][1]:
            copy.wait_recv()
        amount = column[0].astype(F32)
        for i in range(1, planes):
            amount = amount + column[i].astype(F32)
        share(full, me)[...] = amount.astype(BF16)
        for k in range(1, group):
            at = base * steps + group + planes - 2 + k - 1
            sent[name][2].append(
                remote(
                    share(full, me),
                    share(full, me),
                    sem_send.at[at],
                    sem_recv.at[at],
                    in_group(k)[1],
                )
            )

    def spread(amount, target):
        inner = (amount * ADAPTER_SCALE).astype(BF16).astype(F32) * inverse_row
        inner = stack(split(inner))
        for c in range(8):
            cols = slice(c * width // 8, (c + 1) * width // 8)
            out = dot(inner, x[:, cols], NN)
            target[:, cols] = (out[:rank] + out[rank:]).astype(BF16)

    scatter("e")
    spread(total_q[...] * factor, part_q)
    scatter("q")
    pass_hand.wait_recv()
    spread(total_v[...] + hand_in[...], part_v)
    scatter("v")
    for step in (across, gather):
        for name in sums:
            step(name)
    for name in sums:
        for copy in sent[name][2]:
            copy.wait_recv()
    for copy in passed:
        copy.wait_send()
    for name in sums:
        for copies in sent[name]:
            for copy in copies:
                copy.wait_send()


def fused(heads, x, fq, grads, keys, values, scale, qdown, vdown, qup, vup, seqs, planes):
    rows, width = x.shape
    rank = qdown.shape[0]
    half = heads.shape[0] // 2
    group = seqs * CORES
    kv = heads.shape[0]
    used = fq.shape[1] + keys.shape[1]
    unit = group * LANES
    narrow = -(-used // unit) * unit
    operands = (x, fq, grads, keys, values, scale, qdown, vdown, qup, vup)
    vmem = pl.BlockSpec(memory_space=pltpu.VMEM)
    dma = pltpu.SemaphoreType.DMA
    sizes = (narrow, width, width)
    passes = 2 * half + 2
    steps = 3 * (2 * (group - 1) + planes - 1)
    blocks = lambda count: pltpu.VMEM((count, rows, HEAD_SIZE), BF16)
    tile = lambda kind: tuple(
        pltpu.VMEM((n * rows // 2, TOGETHER * rows // 2), kind) for n in (3, 4)
    )

    def held(a):
        if a.shape[1] == width or a.shape[1] == LANES:
            return pltpu.VMEM(a.shape, a.dtype)
        return pltpu.VMEM((kv, a.shape[0], a.shape[1] // kv), a.dtype)

    return pl.pallas_call(
        functools.partial(fused_kernel, seqs, planes),
        in_specs=[pl.BlockSpec(memory_space=pltpu.SMEM)]
        + [pl.BlockSpec(memory_space=pl.ANY)] * len(operands),
        out_specs=[vmem] * 3,
        out_shape=[jax.ShapeDtypeStruct((rank, n), BF16) for n in sizes],
        scratch_shapes=[held(a) for a in operands]
        + [held(values)]
        + [blocks(half), blocks(half), pltpu.VMEM((rank, rows), BF16)] * 2
        + [pltpu.VMEM((rank, rows), F32)] * 2
        + [pltpu.VMEM((rank, n), BF16) for n in sizes]
        + [pltpu.VMEM((group - 1, rank, n // group), BF16) for n in sizes]
        + [pltpu.VMEM((planes, rank, n // group), BF16) for n in sizes]
        + [dma((4 + 6 * kv + CHUNKS,)), dma((passes,)), dma((passes,))]
        + [dma((steps,)), dma((steps,))]
        + [pltpu.VMEM((rows, rank), BF16), pltpu.VMEM((rank, rows), BF16)]
        + [pltpu.VMEM((rank, rows), F32)] * 2
        + [pltpu.VMEM((2 * rows, HEAD_SIZE), F32), pltpu.VMEM((HEAD_SIZE, 2 * rows), BF16)]
        + [tuple(tuple(tile(t) for _ in range(2)) for t in (F32, F32, BF16, BF16))],
        compiler_params=pltpu.CompilerParams(collective_id=0, has_side_effects=True),
        name="fused",
    )(heads, *operands)


def finish_kernel(
    limit,
    heads_ref,
    full_e,
    full_q,
    full_v,
    scale_ref,
    qdown_ref,
    vdown_ref,
    qa_ref,
    qb_ref,
    va_ref,
    vb_ref,
    gain_ref,
):
    rank, width = qa_ref.shape
    kv = vb_ref.shape[1] // HEAD_SIZE
    wide = qb_ref.shape[1] // kv
    used = qb_ref.shape[1] + vb_ref.shape[1]
    squares = jnp.zeros((rank, LANES), F32)
    tops = jnp.zeros((1, LANES), F32)
    for i in range(width // LANES):
        cols = slice(i * LANES, (i + 1) * LANES)
        scale = scale_ref[i : i + 1, :].astype(F32)
        query, value = full_q[:, cols].astype(F32), full_v[:, cols].astype(F32)
        gain = qdown_ref[:, cols].astype(F32) * query + vdown_ref[:, cols].astype(F32) * value
        gain = jnp.sum(gain, axis=0, keepdims=True)
        query, value = query * scale, value * scale
        squares = squares + query * query + value * value
        tops = tops + gain * gain
        qa_ref[:, cols], va_ref[:, cols] = query, value
        gain_ref[i : i + 1, :] = gain
    for i in range(used // LANES):
        piece = full_e[:, i * LANES : (i + 1) * LANES].astype(F32)
        squares = squares + piece * piece
    squares = jnp.sum(squares, axis=0, keepdims=True) + tops
    squares = jnp.sum(squares, axis=1, keepdims=True)
    scale = jnp.minimum(1.0, limit / jnp.sqrt(squares))
    qa_ref[...] = qa_ref[...] * scale
    va_ref[...] = va_ref[...] * scale
    gain_ref[...] = gain_ref[...] * scale
    for pos in range(kv):
        head = heads_ref[pos]
        at = pl.multiple_of(head * wide, HEAD_SIZE)
        qb_ref[:, pl.ds(at, wide)] = full_e[:, pos * wide : (pos + 1) * wide].astype(F32) * scale
        at = pl.multiple_of(head * HEAD_SIZE, HEAD_SIZE)
        first = kv * wide + pos * HEAD_SIZE
        piece = full_e[:, first : first + HEAD_SIZE].astype(F32)
        vb_ref[:, pl.ds(at, HEAD_SIZE)] = piece * scale


def finished(heads, fulls, scale, qdown, vdown, limit, widths):
    rank, width = qdown.shape
    vmem = pl.BlockSpec(memory_space=pltpu.VMEM)
    return pl.pallas_call(
        functools.partial(finish_kernel, limit),
        in_specs=[pl.BlockSpec(memory_space=pltpu.SMEM)] + [vmem] * 6,
        out_specs=[vmem] * (len(widths) + 1),
        out_shape=[jax.ShapeDtypeStruct((rank, w), F32) for w in widths]
        + [jax.ShapeDtypeStruct((width // LANES, LANES), F32)],
        name="finished",
    )(heads, *fulls, scale, qdown, vdown)


def shards(
    layer_input,
    frozen_queries,
    frozen_keys,
    frozen_values,
    output_gradient,
    norm_scale_vector,
    query_down_weight,
    query_up_weight,
    value_down_weight,
    value_up_weight,
    head_ordering,
):
    seqs = lax.axis_size("seq")
    planes = lax.axis_size("dp") // CORES
    rank, width = query_down_weight.shape
    queries = query_up_weight.shape[1]
    kv = value_up_weight.shape[1]
    scale = norm_scale_vector.reshape(width // LANES, LANES)
    fulls = fused(
        head_ordering,
        layer_input[0],
        frozen_queries[0],
        output_gradient[0],
        frozen_keys[0],
        frozen_values[0],
        scale,
        query_down_weight,
        value_down_weight,
        query_up_weight,
        value_up_weight,
        seqs,
        planes,
    )
    limit = math.sqrt(rank * (2 * width + queries + kv) + width)
    qa, qb, va, vb, gain = finished(
        head_ordering,
        fulls,
        scale,
        query_down_weight,
        value_down_weight,
        limit,
        (width, queries, width, kv),
    )
    return (qa, qb, va, vb, gain.reshape(width))


def solution(mesh):
    placed = (
        P("dp", "seq", None),
        P("dp", "seq", None),
        P("dp", "seq", None),
        P("dp", "seq", None),
        P("dp", "seq", None),
        P(),
        P(),
        P(),
        P(),
        P(),
        P(),
    )
    return jax.shard_map(
        shards, mesh=mesh, in_specs=placed, out_specs=(P(), P(), P(), P(), P()), check_vma=False
    )
```

```python
import functools
import math

import jax
import jax.numpy as jnp
from jax import lax
from jax.experimental import pallas as pl
from jax.experimental.pallas import tpu as pltpu
from jax.sharding import PartitionSpec as P

HEAD_SIZE = 128
CORES = 2
LANES = 128
TOGETHER = 8
CHUNKS = 4

EPS = 1e-05
ADAPTER_SCALE = 2.0
F32 = jnp.float32
BF16 = jnp.bfloat16
NT = (((1,), (1,)), ((), ()))
NN = (((1,), (0,)), ((), ()))
MESH = pl.DeviceIdType.MESH


def dot(left, right, dims):
    return lax.dot_general(left, right, dims, preferred_element_type=F32)


def stack(pieces):
    return jnp.concatenate(pieces, axis=0)


def beside(pieces):
    return jnp.concatenate(pieces, axis=1)


def split(value):
    high = value.astype(BF16)
    return high, (value - high.astype(F32)).astype(BF16)


def fused_kernel(
    seqs,
    planes,
    heads_ref,
    x_hbm,
    fq_hbm,
    grad_hbm,
    key_hbm,
    fv_hbm,
    scale_hbm,
    qdown_hbm,
    vdown_hbm,
    qup_hbm,
    vup_hbm,
    full_e,
    full_q,
    full_v,
    x,
    fq,
    grad,
    key,
    fv,
    scale,
    qdown,
    vdown,
    qup,
    vup,
    value,
    key_out,
    value_out,
    mid_out,
    key_in,
    value_in,
    mid_in,
    hand_out,
    hand_in,
    part_e,
    part_q,
    part_v,
    parts_e,
    parts_q,
    parts_v,
    column_e,
    column_q,
    column_v,
    sem_load,
    sem_pass_send,
    sem_pass_recv,
    sem_send,
    sem_recv,
    query_mid,
    query_mid_t,
    total_q,
    total_v,
):
    rows, width = x.shape
    rank = qdown.shape[0]
    kv, _, wide = fq.shape
    half = kv // 2
    per = wide // HEAD_SIZE
    queries = kv * wide
    factor = 1.0 / math.sqrt(HEAD_SIZE)
    group = seqs * CORES
    seq = lax.axis_index("seq")
    place = lax.axis_index("dp")
    plane = place // CORES
    me = seq * CORES + place % CORES
    parity = lax.rem(seq, 2)
    following = {"seq": lax.rem(seq + 1, seqs)}
    previous = {"seq": lax.rem(seq + seqs - 1, seqs)}

    def in_group(k):
        peer = lax.rem(me + k, group)
        return peer, {"seq": peer // CORES, "dp": plane * CORES + peer % CORES}

    def in_column(k):
        return {"dp": lax.rem(plane + k, planes) * CORES + place % CORES}

    loads = []

    def load(source, target):
        copy = pltpu.make_async_copy(source, target, sem_load.at[len(loads)])
        copy.start()
        loads.append(copy)
        return copy

    def by_head(source, target):
        size = target.shape[2]
        return [load(source.at[:, h * size : (h + 1) * size], target.at[h]) for h in range(kv)]

    block = width // CHUNKS
    get_key = by_head(key_hbm, key)
    get_small = [
        load(s, t) for s, t in ((scale_hbm, scale), (qdown_hbm, qdown), (vdown_hbm, vdown))
    ]
    get_x = [
        load(x_hbm.at[:, c * block : (c + 1) * block], x.at[:, c * block : (c + 1) * block])
        for c in range(CHUNKS)
    ]
    get_value = by_head(fv_hbm, fv) + by_head(vup_hbm, vup) + by_head(qup_hbm, qup)
    get_wide = by_head(fq_hbm, fq) + by_head(grad_hbm, grad)

    barrier = pltpu.get_barrier_semaphore()
    for k in range(1, group):
        pl.semaphore_signal(barrier, inc=1, device_id=in_group(k)[1], device_id_type=MESH)
    for k in range(1, planes):
        pl.semaphore_signal(barrier, inc=1, device_id=in_column(k), device_id_type=MESH)

    def remote(source, target, send, recv, device):
        copy = pltpu.make_async_remote_copy(
            src_ref=source,
            dst_ref=target,
            send_sem=send,
            recv_sem=recv,
            device_id=device,
            device_id_type=MESH,
        )
        copy.start()
        return copy

    passed = []

    def hand(source, target, device):
        i = len(passed)
        copy = remote(source, target, sem_pass_send.at[i], sem_pass_recv.at[i], device)
        passed.append(copy)
        return copy

    own_at = lambda i: (1 - parity) * half + i
    prior_at = lambda i: parity * half + i

    for copy in get_key:
        copy.wait()
    for i in range(half):
        key_out[i] = key[heads_ref[own_at(i)]]
    for copy in get_small:
        copy.wait()
    squares = jnp.zeros((rows, LANES), F32)
    each = block // LANES
    for c in range(CHUNKS):
        get_x[c].wait()
        for b in range(c * each, (c + 1) * each):
            part = x[:, b * LANES : (b + 1) * LANES].astype(F32)
            squares = squares + part * part
        if c == 0:
            pl.semaphore_wait(barrier, group + planes - 2)
            pass_key = [hand(key_out.at[i], key_in.at[i], following) for i in range(half)]
    inverse = lax.rsqrt(jnp.sum(squares, axis=1, keepdims=True) * (1.0 / width) + EPS)
    inverse_row = jnp.broadcast_to(inverse, (rows, LANES)).T[:rank]
    mids = [jnp.zeros((rows // 2, 2 * rank), F32)] * 2
    for c in range(CHUNKS):
        cols = slice(c * block, (c + 1) * block)
        down = stack([qdown[:, cols], vdown[:, cols]])
        for r in range(2):
            at = slice(r * rows // 2, (r + 1) * rows // 2)
            normed = []
            for b in range(c * each, (c + 1) * each):
                unit = x[at, b * LANES : (b + 1) * LANES].astype(F32) * inverse[at]
                normed.append((unit * scale[b : b + 1, :].astype(F32)).astype(BF16))
            mids[r] = mids[r] + dot(beside(normed), down, NT)
    mids = stack(mids).astype(BF16)
    twice = (mids * ADAPTER_SCALE).astype(BF16)
    query_mid[...] = twice[:, :rank]
    value_mid = twice[:, rank:]
    eye_r = lax.broadcasted_iota(jnp.int32, (2 * rank, 2 * rank), 0)
    eye_c = lax.broadcasted_iota(jnp.int32, (2 * rank, 2 * rank), 1)
    eye = jnp.where(eye_r == eye_c, ADAPTER_SCALE, 0.0).astype(BF16)
    mids_t = dot(eye, mids, NT)
    query_mid_t[...] = mids_t[:rank].astype(BF16)
    mid_out[...] = mids_t[rank:].astype(BF16)
    for copy in get_value:
        copy.wait()
    for h in range(kv):
        value[h] = (fv[h].astype(F32) + dot(value_mid, vup[h], NN)).astype(BF16)
    for i in range(half):
        value_out[i] = value[heads_ref[own_at(i)]]
    pass_mid = hand(mid_out, mid_in, following)
    pass_value = [hand(value_out.at[i], value_in.at[i], following) for i in range(half)]
    for copy in get_wide:
        copy.wait()

    together = TOGETHER
    groups = per // together
    part_rows = rows // 2
    span = together * part_rows
    log2e = factor * math.log2(math.e)
    total_q[...] = jnp.zeros_like(total_q)
    total_v[...] = jnp.zeros_like(total_v)
    hand_out[...] = jnp.zeros_like(hand_out)
    used = queries + kv * HEAD_SIZE
    if used < part_e.shape[1]:
        part_e[:, used:] = jnp.zeros((rank, part_e.shape[1] - used), BF16)

    def piled(array):
        return stack([array[:, k * HEAD_SIZE : (k + 1) * HEAD_SIZE] for k in range(together)])

    def phase(with_prior):
        before = rows if with_prior else 0
        reaches = [before + part_rows, before + rows]
        place_of = prior_at if with_prior else own_at

        def opened(i, p, a, now):
            head = now["head"]
            at = slice(a * part_rows, (a + 1) * part_rows)
            cols = slice(p * together * HEAD_SIZE, (p + 1) * together * HEAD_SIZE)
            reach = reaches[a]
            adapted = dot(query_mid[at, :], qup[head, :, cols], NN)
            query = (fq[head, at, cols].astype(F32) + adapted).astype(BF16)
            scores = dot(now["keys"][:reach], piled(query), NT)
            return scores, dot(now["values"][:reach], piled(grad[head, at, cols]), NT)

        def weighed(a, scores, dprob):
            key_pos = lax.broadcasted_iota(jnp.int32, (part_rows, span), 0)
            query_pos = lax.broadcasted_iota(jnp.int32, (part_rows, span), 1)
            causal = key_pos <= lax.rem(query_pos, part_rows)
            free = reaches[a] - part_rows
            diagonal = jnp.where(causal, scores[free:], -jnp.inf)
            scores = stack([scores[:free], diagonal]) if free else diagonal
            top = jnp.max(scores, axis=0, keepdims=True)
            exponent = jnp.exp2((scores - top) * log2e)
            probs = exponent * (1.0 / jnp.sum(exponent, axis=0, keepdims=True))
            weights = probs.astype(BF16)
            delta = jnp.sum(weights.astype(F32) * dprob, axis=0, keepdims=True)
            return weights, (probs * (dprob - delta)).astype(BF16)

        def closed(i, p, a, weights, dscore, now):
            pos, head = now["pos"], now["head"]
            cols = slice(p * together * HEAD_SIZE, (p + 1) * together * HEAD_SIZE)
            at = slice(a * part_rows, (a + 1) * part_rows)
            now["term", a] = dot(weights, piled(grad[head, at, cols]), NN)
            now["dq", a] = dot(now["keys_t"][:, : reaches[a]], dscore, NN).astype(BF16)
            if a == 0:
                return
            short, full = now["term", 0], now["term", 1]
            dv = stack([full[: reaches[0]] + short, full[reaches[0] :]])
            if p:
                dv = dv + now["dv"]
            now["dv"] = dv
            dquery = stack(
                [
                    beside(
                        [now["dq", b][:, k * part_rows : (k + 1) * part_rows] for b in range(2)]
                    )
                    for k in range(together)
                ]
            )
            at = pl.multiple_of(pos * wide + p * together * HEAD_SIZE, HEAD_SIZE)
            part_e[:, pl.ds(at, together * HEAD_SIZE)] = (
                dot(query_mid_t[...], dquery, NT) * factor
            ).astype(BF16)
            total_q[...] += dot(qup[head, :, cols], dquery, NN)
            if p < groups - 1:
                return
            up = vup[head]
            mine = dv[before:].astype(BF16)
            raw = dot(mid_out[...], mine, NN)
            total_v[...] += dot(up, mine, NT)
            if before:
                others = dv[:before].astype(BF16)
                raw = raw + dot(mid_in[...], others, NN)
                hand_out[...] += dot(up, others, NT)
            at = pl.multiple_of(queries + pos * HEAD_SIZE, HEAD_SIZE)
            part_e[:, pl.ds(at, HEAD_SIZE)] = raw.astype(BF16)

        def arrived(i):
            for source, target, first in ((key_out, key_in, 0), (value_out, value_in, half + 1)):
                pltpu.make_async_remote_copy(
                    src_ref=source.at[i],
                    dst_ref=target.at[i],
                    send_sem=sem_pass_send.at[first + i],
                    recv_sem=sem_pass_recv.at[first + i],
                    device_id=following,
                    device_id_type=MESH,
                ).wait_recv()

        def body(i, carry):
            if with_prior:
                arrived(i)
            pos = place_of(i)
            head = heads_ref[pos]
            keys, values = key[head], value[head]
            if with_prior:
                keys, values = stack([key_in[i], keys]), stack([value_in[i], values])
            now = {"pos": pos, "head": head, "keys": keys, "values": values, "keys_t": keys.T}
            steps = [(p, a) for p in range(groups) for a in range(2)]
            begun, done = {}, {}
            for t in range(len(steps) + 2):
                if t < len(steps):
                    begun[t] = opened(i, *steps[t], now)
                if 0 <= t - 1 < len(steps):
                    done[t - 1] = weighed(steps[t - 1][1], *begun.pop(t - 1))
                if t >= 2:
                    closed(i, *steps[t - 2], *done.pop(t - 2), now)
            return carry

        if with_prior:
            pass_mid.wait_recv()
        lax.fori_loop(0, half, body, 0)

    phase(False)
    phase(True)
    pass_hand = hand(hand_out, hand_in, previous)

    sums = {
        "e": (part_e, parts_e, column_e, full_e, 0),
        "q": (part_q, parts_q, column_q, full_q, 1),
        "v": (part_v, parts_v, column_v, full_v, 2),
    }
    steps = 2 * (group - 1) + planes - 1
    sent = {name: [[], [], []] for name in sums}

    def share(array, index):
        piece = array.shape[1] // group
        return array.at[:, pl.ds(pl.multiple_of(index * piece, piece), piece)]

    def scatter(name):
        source, parts, _, _, base = sums[name]
        for k in range(1, group):
            peer, device = in_group(k)
            at = base * steps + k - 1
            sent[name][0].append(
                remote(
                    share(source, peer), parts.at[k - 1], sem_send.at[at], sem_recv.at[at], device
                )
            )

    def across(name):
        source, parts, column, _, base = sums[name]
        amount = share(source, me)[...].astype(F32)
        for k in range(1, group):
            sent[name][0][k - 1].wait_recv()
            amount = amount + parts[k - 1].astype(F32)
        column[plane] = amount.astype(BF16)
        for k in range(1, planes):
            at = base * steps + group - 1 + k - 1
            sent[name][1].append(
                remote(
                    column.at[plane],
                    column.at[plane],
                    sem_send.at[at],
                    sem_recv.at[at],
                    in_column(k),
                )
            )

    def gather(name):
        _, _, column, full, base = sums[name]
        for copy in sent[name][1]:
            copy.wait_recv()
        amount = column[0].astype(F32)
        for i in range(1, planes):
            amount = amount + column[i].astype(F32)
        share(full, me)[...] = amount.astype(BF16)
        for k in range(1, group):
            at = base * steps + group + planes - 2 + k - 1
            sent[name][2].append(
                remote(
                    share(full, me),
                    share(full, me),
                    sem_send.at[at],
                    sem_recv.at[at],
                    in_group(k)[1],
                )
            )

    def spread(amount, target):
        inner = (amount * ADAPTER_SCALE).astype(BF16).astype(F32) * inverse_row
        inner = stack(split(inner))
        for c in range(8):
            cols = slice(c * width // 8, (c + 1) * width // 8)
            out = dot(inner, x[:, cols], NN)
            target[:, cols] = (out[:rank] + out[rank:]).astype(BF16)

    scatter("e")
    spread(total_q[...] * factor, part_q)
    scatter("q")
    pass_hand.wait_recv()
    spread(total_v[...] + hand_in[...], part_v)
    scatter("v")
    for step in (across, gather):
        for name in sums:
            step(name)
    for name in sums:
        for copy in sent[name][2]:
            copy.wait_recv()
    for copy in passed:
        copy.wait_send()
    for name in sums:
        for copies in sent[name]:
            for copy in copies:
                copy.wait_send()


def fused(heads, x, fq, grads, keys, values, scale, qdown, vdown, qup, vup, seqs, planes):
    rows, width = x.shape
    rank = qdown.shape[0]
    half = heads.shape[0] // 2
    group = seqs * CORES
    kv = heads.shape[0]
    used = fq.shape[1] + keys.shape[1]
    unit = group * LANES
    narrow = -(-used // unit) * unit
    operands = (x, fq, grads, keys, values, scale, qdown, vdown, qup, vup)
    vmem = pl.BlockSpec(memory_space=pltpu.VMEM)
    dma = pltpu.SemaphoreType.DMA
    sizes = (narrow, width, width)
    passes = 2 * half + 2
    steps = 3 * (2 * (group - 1) + planes - 1)
    blocks = lambda count: pltpu.VMEM((count, rows, HEAD_SIZE), BF16)
    def held(a):
        if a.shape[1] == width or a.shape[1] == LANES:
            return pltpu.VMEM(a.shape, a.dtype)
        return pltpu.VMEM((kv, a.shape[0], a.shape[1] // kv), a.dtype)

    return pl.pallas_call(
        functools.partial(fused_kernel, seqs, planes),
        in_specs=[pl.BlockSpec(memory_space=pltpu.SMEM)]
        + [pl.BlockSpec(memory_space=pl.ANY)] * len(operands),
        out_specs=[vmem] * 3,
        out_shape=[jax.ShapeDtypeStruct((rank, n), BF16) for n in sizes],
        scratch_shapes=[held(a) for a in operands]
        + [held(values)]
        + [blocks(half), blocks(half), pltpu.VMEM((rank, rows), BF16)] * 2
        + [pltpu.VMEM((rank, rows), F32)] * 2
        + [pltpu.VMEM((rank, n), BF16) for n in sizes]
        + [pltpu.VMEM((group - 1, rank, n // group), BF16) for n in sizes]
        + [pltpu.VMEM((planes, rank, n // group), BF16) for n in sizes]
        + [dma((4 + 6 * kv + CHUNKS,)), dma((passes,)), dma((passes,))]
        + [dma((steps,)), dma((steps,))]
        + [pltpu.VMEM((rows, rank), BF16), pltpu.VMEM((rank, rows), BF16)]
        + [pltpu.VMEM((rank, rows), F32)] * 2,
        compiler_params=pltpu.CompilerParams(
            collective_id=0,
            has_side_effects=True,
        ),
        name="fused",
    )(heads, *operands)


def finish_kernel(
    limit,
    heads_ref,
    full_e,
    full_q,
    full_v,
    scale_ref,
    qdown_ref,
    vdown_ref,
    qa_ref,
    qb_ref,
    va_ref,
    vb_ref,
    gain_ref,
):
    rank, width = qa_ref.shape
    kv = vb_ref.shape[1] // HEAD_SIZE
    wide = qb_ref.shape[1] // kv
    used = qb_ref.shape[1] + vb_ref.shape[1]
    squares = jnp.zeros((rank, LANES), F32)
    tops = jnp.zeros((1, LANES), F32)
    for i in range(width // LANES):
        cols = slice(i * LANES, (i + 1) * LANES)
        scale = scale_ref[i : i + 1, :].astype(F32)
        query, value = full_q[:, cols].astype(F32), full_v[:, cols].astype(F32)
        gain = qdown_ref[:, cols].astype(F32) * query + vdown_ref[:, cols].astype(F32) * value
        gain = jnp.sum(gain, axis=0, keepdims=True)
        query, value = query * scale, value * scale
        squares = squares + query * query + value * value
        tops = tops + gain * gain
        qa_ref[:, cols], va_ref[:, cols] = query, value
        gain_ref[i : i + 1, :] = gain
    for i in range(used // LANES):
        piece = full_e[:, i * LANES : (i + 1) * LANES].astype(F32)
        squares = squares + piece * piece
    squares = jnp.sum(squares, axis=0, keepdims=True) + tops
    squares = jnp.sum(squares, axis=1, keepdims=True)
    scale = jnp.minimum(1.0, limit / jnp.sqrt(squares))
    qa_ref[...] = qa_ref[...] * scale
    va_ref[...] = va_ref[...] * scale
    gain_ref[...] = gain_ref[...] * scale
    for pos in range(kv):
        head = heads_ref[pos]
        at = pl.multiple_of(head * wide, HEAD_SIZE)
        qb_ref[:, pl.ds(at, wide)] = full_e[:, pos * wide : (pos + 1) * wide].astype(F32) * scale
        at = pl.multiple_of(head * HEAD_SIZE, HEAD_SIZE)
        first = kv * wide + pos * HEAD_SIZE
        piece = full_e[:, first : first + HEAD_SIZE].astype(F32)
        vb_ref[:, pl.ds(at, HEAD_SIZE)] = piece * scale


def finished(heads, fulls, scale, qdown, vdown, limit, widths):
    rank, width = qdown.shape
    vmem = pl.BlockSpec(memory_space=pltpu.VMEM)
    return pl.pallas_call(
        functools.partial(finish_kernel, limit),
        in_specs=[pl.BlockSpec(memory_space=pltpu.SMEM)] + [vmem] * 6,
        out_specs=[vmem] * (len(widths) + 1),
        out_shape=[jax.ShapeDtypeStruct((rank, w), F32) for w in widths]
        + [jax.ShapeDtypeStruct((width // LANES, LANES), F32)],
        name="finished",
    )(heads, *fulls, scale, qdown, vdown)


def shards(
    layer_input,
    frozen_queries,
    frozen_keys,
    frozen_values,
    output_gradient,
    norm_scale_vector,
    query_down_weight,
    query_up_weight,
    value_down_weight,
    value_up_weight,
    head_ordering,
):
    seqs = lax.axis_size("seq")
    planes = lax.axis_size("dp") // CORES
    rank, width = query_down_weight.shape
    queries = query_up_weight.shape[1]
    kv = value_up_weight.shape[1]
    scale = norm_scale_vector.reshape(width // LANES, LANES)
    fulls = fused(
        head_ordering,
        layer_input[0],
        frozen_queries[0],
        output_gradient[0],
        frozen_keys[0],
        frozen_values[0],
        scale,
        query_down_weight,
        value_down_weight,
        query_up_weight,
        value_up_weight,
        seqs,
        planes,
    )
    limit = math.sqrt(rank * (2 * width + queries + kv) + width)
    qa, qb, va, vb, gain = finished(
        head_ordering,
        fulls,
        scale,
        query_down_weight,
        value_down_weight,
        limit,
        (width, queries, width, kv),
    )
    return (qa, qb, va, vb, gain.reshape(width))


def solution(mesh):
    placed = (
        P("dp", "seq", None),
        P("dp", "seq", None),
        P("dp", "seq", None),
        P("dp", "seq", None),
        P("dp", "seq", None),
        P(),
        P(),
        P(),
        P(),
        P(),
        P(),
    )
    return jax.shard_map(
        shards, mesh=mesh, in_specs=placed, out_specs=(P(), P(), P(), P(), P()), check_vma=False
    )
```

```python
import functools
import math

import jax
import jax.numpy as jnp
from jax import lax
from jax.experimental import pallas as pl
from jax.experimental.pallas import tpu as pltpu
from jax.sharding import PartitionSpec as P

HEAD_SIZE = 128
CORES = 2
LANES = 128
TOGETHER = 8
CHUNKS = 4
PIECES = 1

EPS = 1e-05
ADAPTER_SCALE = 2.0
F32 = jnp.float32
BF16 = jnp.bfloat16
NT = (((1,), (1,)), ((), ()))
NN = (((1,), (0,)), ((), ()))
MESH = pl.DeviceIdType.MESH


def dot(left, right, dims):
    return lax.dot_general(left, right, dims, preferred_element_type=F32)


def stack(pieces):
    return jnp.concatenate(pieces, axis=0)


def beside(pieces):
    return jnp.concatenate(pieces, axis=1)


def split(value):
    high = value.astype(BF16)
    return high, (value - high.astype(F32)).astype(BF16)


def early_columns(kv, wide, group):
    unit = group * LANES
    return -(-2 * (kv // 2 - 1) * wide // unit) * unit


def fused_kernel(
    seqs,
    planes,
    heads_hbm,
    x_hbm,
    fq_hbm,
    grad_hbm,
    key_hbm,
    fv_hbm,
    scale_hbm,
    qdown_hbm,
    vdown_hbm,
    qup_hbm,
    vup_hbm,
    full_e,
    full_s,
    x,
    fq,
    grad,
    key,
    fv,
    scale,
    qdown,
    vdown,
    qup,
    vup,
    value,
    key_out,
    value_out,
    mid_out,
    key_in,
    value_in,
    mid_in,
    hand_out,
    hand_in,
    part_e,
    part_s,
    parts,
    columns,
    sem_load,
    sem_pass_send,
    sem_pass_recv,
    sem_send,
    sem_recv,
    query_mid,
    query_mid_t,
    total_q,
    total_v,
    heads_ref,
):
    rows, width = x.shape
    rank = qdown.shape[0]
    kv, _, wide = fq.shape
    half = kv // 2
    per = wide // HEAD_SIZE
    queries = kv * wide
    factor = 1.0 / math.sqrt(HEAD_SIZE)
    group = seqs * CORES
    seq = lax.axis_index("seq")
    place = lax.axis_index("dp")
    plane = place // CORES
    me = seq * CORES + place % CORES
    parity = lax.rem(seq, 2)
    following = {"seq": lax.rem(seq + 1, seqs)}
    previous = {"seq": lax.rem(seq + seqs - 1, seqs)}

    def in_group(k):
        peer = lax.rem(me + k, group)
        return peer, {"seq": peer // CORES, "dp": plane * CORES + peer % CORES}

    def in_column(k):
        return {"dp": lax.rem(plane + k, planes) * CORES + place % CORES}

    loads = []

    def load(source, target):
        copy = pltpu.make_async_copy(source, target, sem_load.at[len(loads)])
        copy.start()
        loads.append(copy)
        return copy

    def by_head(source, target):
        size = target.shape[2]
        return [load(source.at[:, h * size : (h + 1) * size], target.at[h]) for h in range(kv)]

    block = width // CHUNKS
    get_key = [load(heads_hbm, heads_ref)] + by_head(key_hbm, key)
    get_small = [
        load(s, t) for s, t in ((scale_hbm, scale), (qdown_hbm, qdown), (vdown_hbm, vdown))
    ]
    get_x = [
        load(x_hbm.at[:, c * block : (c + 1) * block], x.at[:, c * block : (c + 1) * block])
        for c in range(CHUNKS)
    ]
    get_value = by_head(fv_hbm, fv) + by_head(vup_hbm, vup) + by_head(qup_hbm, qup)
    get_wide = by_head(fq_hbm, fq) + by_head(grad_hbm, grad)

    barrier = pltpu.get_barrier_semaphore()
    for k in range(1, group):
        pl.semaphore_signal(barrier, inc=1, device_id=in_group(k)[1], device_id_type=MESH)
    for k in range(1, planes):
        pl.semaphore_signal(barrier, inc=1, device_id=in_column(k), device_id_type=MESH)

    def remote(source, target, send, recv, device):
        copy = pltpu.make_async_remote_copy(
            src_ref=source,
            dst_ref=target,
            send_sem=send,
            recv_sem=recv,
            device_id=device,
            device_id_type=MESH,
        )
        copy.start()
        return copy

    def handing(source, target, device, at):
        return pltpu.make_async_remote_copy(
            src_ref=source,
            dst_ref=target,
            send_sem=sem_pass_send.at[at],
            recv_sem=sem_pass_recv.at[at],
            device_id=device,
            device_id_type=MESH,
        )

    key_copy = lambda i: handing(key_out.at[i], key_in.at[i], following, i)
    value_copy = lambda i: handing(value_out.at[i], value_in.at[i], following, half + i)
    pass_mid = handing(mid_out, mid_in, following, 2 * half)
    pass_hand = handing(hand_out, hand_in, previous, 2 * half + 1)

    own_at = lambda i: (1 - parity) * half + i
    prior_at = lambda i: parity * half + i

    for copy in get_key:
        copy.wait()
    for i in range(half):
        key_out[i] = key[heads_ref[own_at(i)]]
    for copy in get_small:
        copy.wait()
    squares = jnp.zeros((rows, LANES), F32)
    each = block // LANES
    for c in range(CHUNKS):
        get_x[c].wait()
        for b in range(c * each, (c + 1) * each):
            part = x[:, b * LANES : (b + 1) * LANES].astype(F32)
            squares = squares + part * part
        if c == 0:
            pl.semaphore_wait(barrier, group + planes - 2)
            for i in range(half - 1):
                key_copy(i).start()
    inverse = lax.rsqrt(jnp.sum(squares, axis=1, keepdims=True) * (1.0 / width) + EPS)
    inverse_row = jnp.broadcast_to(inverse, (rows, LANES)).T[: 2 * rank]
    mids = [jnp.zeros((rows // 2, 2 * rank), F32)] * 2
    for c in range(CHUNKS):
        cols = slice(c * block, (c + 1) * block)
        down = stack([qdown[:, cols], vdown[:, cols]])
        for r in range(2):
            at = slice(r * rows // 2, (r + 1) * rows // 2)
            normed = []
            for b in range(c * each, (c + 1) * each):
                unit = x[at, b * LANES : (b + 1) * LANES].astype(F32) * inverse[at]
                normed.append((unit * scale[b : b + 1, :].astype(F32)).astype(BF16))
            mids[r] = mids[r] + dot(beside(normed), down, NT)
    mids = stack(mids).astype(BF16)
    twice = (mids * ADAPTER_SCALE).astype(BF16)
    query_mid[...] = twice[:, :rank]
    value_mid = twice[:, rank:]
    eye_r = lax.broadcasted_iota(jnp.int32, (2 * rank, 2 * rank), 0)
    eye_c = lax.broadcasted_iota(jnp.int32, (2 * rank, 2 * rank), 1)
    eye = jnp.where(eye_r == eye_c, ADAPTER_SCALE, 0.0).astype(BF16)
    mids_t = dot(eye, mids, NT)
    query_mid_t[...] = mids_t[:rank].astype(BF16)
    mid_out[...] = mids_t[rank:].astype(BF16)
    for copy in get_value:
        copy.wait()
    for h in range(kv):
        value[h] = (fv[h].astype(F32) + dot(value_mid, vup[h], NN)).astype(BF16)
    for i in range(half):
        value_out[i] = value[heads_ref[own_at(i)]]
    pass_mid.start()
    for copy in get_wide:
        copy.wait()

    together = TOGETHER
    groups = per // together
    part_rows = rows // 2
    span = together * part_rows
    log2e = factor * math.log2(math.e)
    total_q[...] = jnp.zeros_like(total_q)
    total_v[...] = jnp.zeros_like(total_v)
    hand_out[...] = jnp.zeros_like(hand_out)
    lead = half - 1
    early = early_columns(kv, wide, group)
    narrow = early + (2 * wide + kv * HEAD_SIZE)
    if 2 * lead * wide < early:
        part_e[:, 2 * lead * wide : early] = jnp.zeros((rank, early - 2 * lead * wide), BF16)
    if narrow < part_e.shape[1]:
        part_e[:, narrow:] = jnp.zeros((rank, part_e.shape[1] - narrow), BF16)

    def slot_of(with_prior, i):
        side = parity if with_prior else 1 - parity
        last = i // lead
        return (1 - last) * (side * lead + i) * wide + last * (early + side * wide)

    def piled(array):
        return stack([array[:, k * HEAD_SIZE : (k + 1) * HEAD_SIZE] for k in range(together)])

    def phase(with_prior, start, stop):
        before = rows if with_prior else 0
        reaches = [before + part_rows, before + rows]
        place_of = prior_at if with_prior else own_at

        def opened(i, p, a, now):
            head = now["head"]
            at = slice(a * part_rows, (a + 1) * part_rows)
            cols = slice(p * together * HEAD_SIZE, (p + 1) * together * HEAD_SIZE)
            reach = reaches[a]
            adapted = dot(query_mid[at, :], qup[head, :, cols], NN)
            query = (fq[head, at, cols].astype(F32) + adapted).astype(BF16)
            scores = dot(now["keys"][:reach], piled(query), NT)
            return scores, dot(now["values"][:reach], piled(grad[head, at, cols]), NT)

        def weighed(a, scores, dprob):
            key_pos = lax.broadcasted_iota(jnp.int32, (part_rows, span), 0)
            query_pos = lax.broadcasted_iota(jnp.int32, (part_rows, span), 1)
            causal = key_pos <= lax.rem(query_pos, part_rows)
            free = reaches[a] - part_rows
            diagonal = jnp.where(causal, scores[free:], -jnp.inf)
            scores = stack([scores[:free], diagonal]) if free else diagonal
            top = jnp.max(scores, axis=0, keepdims=True)
            exponent = jnp.exp2((scores - top) * log2e)
            probs = exponent * (1.0 / jnp.sum(exponent, axis=0, keepdims=True))
            weights = probs.astype(BF16)
            delta = jnp.sum(probs * dprob, axis=0, keepdims=True)
            return weights, (probs * (dprob - delta)).astype(BF16)

        def closed(i, p, a, weights, dscore, now):
            pos, head = now["pos"], now["head"]
            cols = slice(p * together * HEAD_SIZE, (p + 1) * together * HEAD_SIZE)
            at = slice(a * part_rows, (a + 1) * part_rows)
            now["term", a] = dot(weights, piled(grad[head, at, cols]), NN)
            now["dq", a] = dot(now["keys_t"][:, : reaches[a]], dscore, NN).astype(BF16)
            if a == 0:
                return
            short, full = now["term", 0], now["term", 1]
            dv = stack([full[: reaches[0]] + short, full[reaches[0] :]])
            if p:
                dv = dv + now["dv"]
            now["dv"] = dv
            dquery = stack(
                [
                    beside(
                        [now["dq", b][:, k * part_rows : (k + 1) * part_rows] for b in range(2)]
                    )
                    for k in range(together)
                ]
            )
            at = slot_of(with_prior, i) + p * together * HEAD_SIZE
            at = pl.multiple_of(at, HEAD_SIZE)
            part_e[:, pl.ds(at, together * HEAD_SIZE)] = (
                dot(query_mid_t[...], dquery, NT) * factor
            ).astype(BF16)
            total_q[...] += dot(qup[head, :, cols], dquery, NN)
            if p < groups - 1:
                return
            up = vup[head]
            mine = dv[before:].astype(BF16)
            raw = dot(mid_out[...], mine, NN)
            total_v[...] += dot(up, mine, NT)
            if before:
                others = dv[:before].astype(BF16)
                raw = raw + dot(mid_in[...], others, NN)
                hand_out[...] += dot(up, others, NT)
            at = pl.multiple_of(early + 2 * wide + pos * HEAD_SIZE, HEAD_SIZE)
            part_e[:, pl.ds(at, HEAD_SIZE)] = raw.astype(BF16)

        def arrived(i):
            key_copy(i).wait_recv()
            value_copy(i).wait_recv()

        def body(i, carry):
            if with_prior:
                arrived(i)
            elif start == 0:
                value_copy(i).start()
            pos = place_of(i)
            head = heads_ref[pos]
            keys, values = key[head], value[head]
            if with_prior:
                keys, values = stack([key_in[i], keys]), stack([value_in[i], values])
            now = {"pos": pos, "head": head, "keys": keys, "values": values, "keys_t": keys.T}
            steps = [(p, a) for p in range(groups) for a in range(2)]
            begun, done = {}, {}
            for t in range(len(steps) + 2):
                if t < len(steps):
                    begun[t] = opened(i, *steps[t], now)
                if 0 <= t - 1 < len(steps):
                    done[t - 1] = weighed(steps[t - 1][1], *begun.pop(t - 1))
                if t >= 2:
                    closed(i, *steps[t - 2], *done.pop(t - 2), now)
            return carry

        if with_prior:
            pass_mid.wait_recv()
        lax.fori_loop(start, stop, body, 0)

    phase(False, 0, half - 1)
    key_copy(half - 1).start()
    value_copy(half - 1).start()
    phase(True, 0, half)

    late = part_e.shape[1] - early
    each = width // PIECES
    sums = [(part_e, full_e, 0, early), (part_e, full_e, early, late)]
    sums += [(part_s, full_s, c * each, each) for c in range(PIECES)]
    steps = 2 * (group - 1) + planes - 1
    sent = [[[], [], []] for _ in sums]

    def share(array, at, size, index):
        piece = size // group
        return array.at[:, pl.ds(pl.multiple_of(at + index * piece, LANES), piece)]

    def scatter(c):
        source, _, start, size = sums[c]
        for k in range(1, group):
            peer, device = in_group(k)
            at = c * steps + k - 1
            sent[c][0].append(
                remote(
                    share(source, start, size, peer),
                    parts[c].at[k - 1],
                    sem_send.at[at],
                    sem_recv.at[at],
                    device,
                )
            )

    def across(c):
        source, _, start, size = sums[c]
        column = columns[c]
        amount = share(source, start, size, me)[...].astype(F32)
        for k in range(1, group):
            sent[c][0][k - 1].wait_recv()
            amount = amount + parts[c][k - 1].astype(F32)
        column[plane] = amount.astype(BF16)
        for k in range(1, planes):
            at = c * steps + group - 1 + k - 1
            sent[c][1].append(
                remote(
                    column.at[plane],
                    column.at[plane],
                    sem_send.at[at],
                    sem_recv.at[at],
                    in_column(k),
                )
            )

    def gather(c):
        _, full, start, size = sums[c]
        for copy in sent[c][1]:
            copy.wait_recv()
        amount = columns[c][0].astype(F32)
        for i in range(1, planes):
            amount = amount + columns[c][i].astype(F32)
        share(full, start, size, me)[...] = amount.astype(BF16)
        for k in range(1, group):
            at = c * steps + group + planes - 2 + k - 1
            sent[c][2].append(
                remote(
                    share(full, start, size, me),
                    share(full, start, size, me),
                    sem_send.at[at],
                    sem_recv.at[at],
                    in_group(k)[1],
                )
            )

    pass_hand.start()
    scatter(0)
    phase(False, half - 1, half)
    scatter(1)
    pass_hand.wait_recv()
    inner = stack([total_q[...] * factor, total_v[...] + hand_in[...]]) * ADAPTER_SCALE
    inner = stack(split(inner.astype(BF16).astype(F32) * inverse_row))
    for c in range(PIECES):
        cols = slice(c * each, (c + 1) * each)
        out = dot(inner, x[:, cols], NN)
        part_s[:, cols] = (out[: 2 * rank] + out[2 * rank :]).astype(BF16)
        scatter(2 + c)
        if c == 0:
            across(0)
    across(1)
    gather(0)
    for c in range(PIECES):
        across(2 + c)
        if c == 0:
            gather(1)
    for c in range(PIECES):
        gather(2 + c)
    for group_sent in sent:
        for copy in group_sent[2]:
            copy.wait_recv()
    for i in range(half):
        key_copy(i).wait_send()
        value_copy(i).wait_send()
    pass_mid.wait_send()
    pass_hand.wait_send()
    for group_sent in sent:
        for copies in group_sent:
            for copy in copies:
                copy.wait_send()


def fused(heads, x, fq, grads, keys, values, scale, qdown, vdown, qup, vup, seqs, planes):
    rows, width = x.shape
    rank = qdown.shape[0]
    half = heads.shape[0] // 2
    group = seqs * CORES
    kv = heads.shape[0]
    wide = fq.shape[1] // kv
    unit = group * LANES
    early = early_columns(kv, wide, group)
    late = -(-(2 * wide + keys.shape[1]) // unit) * unit
    operands = (x, fq, grads, keys, values, scale, qdown, vdown, qup, vup)
    vmem = pl.BlockSpec(memory_space=pltpu.VMEM)
    dma = pltpu.SemaphoreType.DMA
    sizes = ((rank, early + late), (2 * rank, width))
    cuts = ((rank, early), (rank, late)) + ((2 * rank, width // PIECES),) * PIECES
    passes = 2 * half + 2
    steps = len(cuts) * (2 * (group - 1) + planes - 1)
    blocks = lambda count: pltpu.VMEM((count, rows, HEAD_SIZE), BF16)
    def held(a):
        if a.shape[1] == width or a.shape[1] == LANES:
            return pltpu.VMEM(a.shape, a.dtype)
        return pltpu.VMEM((kv, a.shape[0], a.shape[1] // kv), a.dtype)

    return pl.pallas_call(
        functools.partial(fused_kernel, seqs, planes),
        in_specs=[pl.BlockSpec(memory_space=pltpu.HBM)] * (1 + len(operands)),
        out_specs=[vmem] * 2,
        out_shape=[jax.ShapeDtypeStruct(n, BF16) for n in sizes],
        scratch_shapes=[held(a) for a in operands]
        + [held(values)]
        + [blocks(half), blocks(half), pltpu.VMEM((rank, rows), BF16)] * 2
        + [pltpu.VMEM((rank, rows), F32)] * 2
        + [pltpu.VMEM(n, BF16) for n in sizes]
        + [tuple(pltpu.VMEM((group - 1, r, n // group), BF16) for r, n in cuts)]
        + [tuple(pltpu.VMEM((planes, r, n // group), BF16) for r, n in cuts)]
        + [dma((5 + 6 * kv + CHUNKS,)), dma((passes,)), dma((passes,))]
        + [dma((steps,)), dma((steps,))]
        + [pltpu.VMEM((rows, rank), BF16), pltpu.VMEM((rank, rows), BF16)]
        + [pltpu.VMEM((rank, rows), F32)] * 2
        + [pltpu.SMEM((kv,), jnp.int32)],
        compiler_params=pltpu.CompilerParams(
            collective_id=0,
            has_side_effects=True,
        ),
        name="fused",
    )(heads, *operands)


def finish_kernel(
    limit,
    early,
    heads_ref,
    full_e,
    full_s,
    scale_ref,
    qdown_ref,
    vdown_ref,
    qa_ref,
    qb_ref,
    va_ref,
    vb_ref,
    gain_ref,
):
    rank, width = qa_ref.shape
    kv = vb_ref.shape[1] // HEAD_SIZE
    wide = qb_ref.shape[1] // kv
    lead = kv // 2 - 1
    starts = []
    for pos in range(kv):
        side, i = pos // (lead + 1), pos % (lead + 1)
        starts.append(early + side * wide if i == lead else (side * lead + i) * wide)
    behind = early + 2 * wide
    squares = jnp.zeros((rank, LANES), F32)
    tops = jnp.zeros((1, LANES), F32)
    for i in range(width // LANES):
        cols = slice(i * LANES, (i + 1) * LANES)
        scale = scale_ref[i : i + 1, :].astype(F32)
        both = full_s[:, cols].astype(F32)
        query, value = both[:rank], both[rank:]
        gain = qdown_ref[:, cols].astype(F32) * query + vdown_ref[:, cols].astype(F32) * value
        gain = jnp.sum(gain, axis=0, keepdims=True)
        query, value = query * scale, value * scale
        squares = squares + query * query + value * value
        tops = tops + gain * gain
        qa_ref[:, cols], va_ref[:, cols] = query, value
        gain_ref[i : i + 1, :] = gain
    spans = [(start, wide) for start in starts] + [(behind, vb_ref.shape[1])]
    for start, size in spans:
        for i in range(size // LANES):
            piece = full_e[:, start + i * LANES : start + (i + 1) * LANES].astype(F32)
            squares = squares + piece * piece
    squares = jnp.sum(squares, axis=0, keepdims=True) + tops
    squares = jnp.sum(squares, axis=1, keepdims=True)
    scale = jnp.minimum(1.0, limit / jnp.sqrt(squares))
    qa_ref[...] = qa_ref[...] * scale
    va_ref[...] = va_ref[...] * scale
    gain_ref[...] = gain_ref[...] * scale
    for pos in range(kv):
        head = heads_ref[pos]
        at = pl.multiple_of(head * wide, HEAD_SIZE)
        qb_ref[:, pl.ds(at, wide)] = full_e[:, starts[pos] : starts[pos] + wide].astype(F32) * scale
        at = pl.multiple_of(head * HEAD_SIZE, HEAD_SIZE)
        first = behind + pos * HEAD_SIZE
        piece = full_e[:, first : first + HEAD_SIZE].astype(F32)
        vb_ref[:, pl.ds(at, HEAD_SIZE)] = piece * scale


def finished(heads, fulls, scale, qdown, vdown, limit, early, widths):
    rank, width = qdown.shape
    vmem = pl.BlockSpec(memory_space=pltpu.VMEM)
    return pl.pallas_call(
        functools.partial(finish_kernel, limit, early),
        in_specs=[pl.BlockSpec(memory_space=pltpu.SMEM)] + [vmem] * 5,
        out_specs=[vmem] * (len(widths) + 1),
        out_shape=[jax.ShapeDtypeStruct((rank, w), F32) for w in widths]
        + [jax.ShapeDtypeStruct((width // LANES, LANES), F32)],

        name="finished",
    )(heads, *fulls, scale, qdown, vdown)


def shards(
    layer_input,
    frozen_queries,
    frozen_keys,
    frozen_values,
    output_gradient,
    norm_scale_vector,
    query_down_weight,
    query_up_weight,
    value_down_weight,
    value_up_weight,
    head_ordering,
):
    seqs = lax.axis_size("seq")
    planes = lax.axis_size("dp") // CORES
    rank, width = query_down_weight.shape
    queries = query_up_weight.shape[1]
    kv = value_up_weight.shape[1]
    scale = norm_scale_vector.reshape(width // LANES, LANES)
    fulls = fused(
        head_ordering,
        layer_input[0],
        frozen_queries[0],
        output_gradient[0],
        frozen_keys[0],
        frozen_values[0],
        scale,
        query_down_weight,
        value_down_weight,
        query_up_weight,
        value_up_weight,
        seqs,
        planes,
    )
    limit = math.sqrt(rank * (2 * width + queries + kv) + width)
    qa, qb, va, vb, gain = finished(
        head_ordering,
        fulls,
        scale,
        query_down_weight,
        value_down_weight,
        limit,
        early_columns(head_ordering.shape[0], queries // head_ordering.shape[0], seqs * CORES),
        (width, queries, width, kv),
    )
    return (qa, qb, va, vb, gain.reshape(width))


def solution(mesh):
    placed = (
        P("dp", "seq", None),
        P("dp", "seq", None),
        P("dp", "seq", None),
        P("dp", "seq", None),
        P("dp", "seq", None),
        P(),
        P(),
        P(),
        P(),
        P(),
        P(),
    )
    return jax.shard_map(
        shards, mesh=mesh, in_specs=placed, out_specs=(P(), P(), P(), P(), P()), check_vma=False
    )
```

```python
import functools
import math

import jax
import jax.numpy as jnp
from jax import lax
from jax.experimental import pallas as pl
from jax.experimental.pallas import tpu as pltpu
from jax.sharding import PartitionSpec as P

HEAD_SIZE = 128
CORES = 2
LANES = 128
TOGETHER = 8
CHUNKS = 4
PIECES = 2

EPS = 1e-05
ADAPTER_SCALE = 2.0
F32 = jnp.float32
BF16 = jnp.bfloat16
NT = (((1,), (1,)), ((), ()))
NN = (((1,), (0,)), ((), ()))
MESH = pl.DeviceIdType.MESH


def dot(left, right, dims):
    return lax.dot_general(left, right, dims, preferred_element_type=F32)


def stack(pieces):
    return jnp.concatenate(pieces, axis=0)


def beside(pieces):
    return jnp.concatenate(pieces, axis=1)


def split(value):
    high = value.astype(BF16)
    return high, (value - high.astype(F32)).astype(BF16)


def early_columns(kv, wide, group):
    unit = group * LANES
    return -(-2 * (kv // 2 - 1) * wide // unit) * unit


def fused_kernel(
    seqs,
    planes,
    heads_hbm,
    x_hbm,
    fq_hbm,
    grad_hbm,
    key_hbm,
    fv_hbm,
    scale_hbm,
    qdown_hbm,
    vdown_hbm,
    qup_hbm,
    vup_hbm,
    full_e,
    full_s,
    x,
    fq,
    grad,
    key,
    fv,
    scale,
    qdown,
    vdown,
    qup,
    vup,
    value,
    key_out,
    value_out,
    mid_out,
    key_in,
    value_in,
    mid_in,
    hand_out,
    hand_in,
    part_e,
    part_s,
    parts,
    columns,
    sem_load,
    sem_pass_send,
    sem_pass_recv,
    sem_send,
    sem_recv,
    query_mid,
    query_mid_t,
    total_q,
    total_v,
    heads_ref,
):
    rows, width = x.shape
    rank = qdown.shape[0]
    kv, _, wide = fq.shape
    half = kv // 2
    per = wide // HEAD_SIZE
    queries = kv * wide
    factor = 1.0 / math.sqrt(HEAD_SIZE)
    group = seqs * CORES
    seq = lax.axis_index("seq")
    place = lax.axis_index("dp")
    plane = place // CORES
    me = seq * CORES + place % CORES
    parity = lax.rem(seq, 2)
    following = {"seq": lax.rem(seq + 1, seqs)}
    previous = {"seq": lax.rem(seq + seqs - 1, seqs)}

    def in_group(k):
        peer = lax.rem(me + k, group)
        return peer, {"seq": peer // CORES, "dp": plane * CORES + peer % CORES}

    def in_column(k):
        return {"dp": lax.rem(plane + k, planes) * CORES + place % CORES}

    loads = []

    def load(source, target):
        copy = pltpu.make_async_copy(source, target, sem_load.at[len(loads)])
        copy.start()
        loads.append(copy)
        return copy

    def by_head(source, target):
        size = target.shape[2]
        return [load(source.at[:, h * size : (h + 1) * size], target.at[h]) for h in range(kv)]

    block = width // CHUNKS
    get_key = [load(heads_hbm, heads_ref)] + by_head(key_hbm, key)
    get_small = [
        load(s, t) for s, t in ((scale_hbm, scale), (qdown_hbm, qdown), (vdown_hbm, vdown))
    ]
    get_x = [
        load(x_hbm.at[:, c * block : (c + 1) * block], x.at[:, c * block : (c + 1) * block])
        for c in range(CHUNKS)
    ]
    get_value = by_head(fv_hbm, fv) + by_head(vup_hbm, vup) + by_head(qup_hbm, qup)
    get_wide = by_head(fq_hbm, fq) + by_head(grad_hbm, grad)

    barrier = pltpu.get_barrier_semaphore()
    for k in range(1, group):
        pl.semaphore_signal(barrier, inc=1, device_id=in_group(k)[1], device_id_type=MESH)
    for k in range(1, planes):
        pl.semaphore_signal(barrier, inc=1, device_id=in_column(k), device_id_type=MESH)

    def remote(source, target, send, recv, device):
        copy = pltpu.make_async_remote_copy(
            src_ref=source,
            dst_ref=target,
            send_sem=send,
            recv_sem=recv,
            device_id=device,
            device_id_type=MESH,
        )
        copy.start()
        return copy

    def handing(source, target, device, at):
        return pltpu.make_async_remote_copy(
            src_ref=source,
            dst_ref=target,
            send_sem=sem_pass_send.at[at],
            recv_sem=sem_pass_recv.at[at],
            device_id=device,
            device_id_type=MESH,
        )

    key_copy = lambda i: handing(key_out.at[i], key_in.at[i], following, i)
    value_copy = lambda i: handing(value_out.at[i], value_in.at[i], following, half + i)
    pass_mid = handing(mid_out, mid_in, following, 2 * half)
    pass_hand = handing(hand_out, hand_in, previous, 2 * half + 1)

    own_at = lambda i: (1 - parity) * half + i
    prior_at = lambda i: parity * half + i

    for copy in get_key:
        copy.wait()
    for i in range(half):
        key_out[i] = key[heads_ref[own_at(i)]]
    for copy in get_small:
        copy.wait()
    squares = jnp.zeros((rows, LANES), F32)
    each = block // LANES
    for c in range(CHUNKS):
        get_x[c].wait()
        for b in range(c * each, (c + 1) * each):
            part = x[:, b * LANES : (b + 1) * LANES].astype(F32)
            squares = squares + part * part
        if c == 0:
            pl.semaphore_wait(barrier, group + planes - 2)
            for i in range(half - 1):
                key_copy(i).start()
    inverse = lax.rsqrt(jnp.sum(squares, axis=1, keepdims=True) * (1.0 / width) + EPS)
    inverse_row = jnp.broadcast_to(inverse, (rows, LANES)).T[: 2 * rank]
    mids = [jnp.zeros((rows // 2, 2 * rank), F32)] * 2
    for c in range(CHUNKS):
        cols = slice(c * block, (c + 1) * block)
        down = stack([qdown[:, cols], vdown[:, cols]])
        for r in range(2):
            at = slice(r * rows // 2, (r + 1) * rows // 2)
            normed = []
            for b in range(c * each, (c + 1) * each):
                unit = x[at, b * LANES : (b + 1) * LANES].astype(F32) * inverse[at]
                normed.append((unit * scale[b : b + 1, :].astype(F32)).astype(BF16))
            mids[r] = mids[r] + dot(beside(normed), down, NT)
    mids = stack(mids).astype(BF16)
    twice = (mids * ADAPTER_SCALE).astype(BF16)
    query_mid[...] = twice[:, :rank]
    value_mid = twice[:, rank:]
    eye_r = lax.broadcasted_iota(jnp.int32, (2 * rank, 2 * rank), 0)
    eye_c = lax.broadcasted_iota(jnp.int32, (2 * rank, 2 * rank), 1)
    eye = jnp.where(eye_r == eye_c, ADAPTER_SCALE, 0.0).astype(BF16)
    mids_t = dot(eye, mids, NT)
    query_mid_t[...] = mids_t[:rank].astype(BF16)
    mid_out[...] = mids_t[rank:].astype(BF16)
    for copy in get_value:
        copy.wait()
    for h in range(kv):
        value[h] = (fv[h].astype(F32) + dot(value_mid, vup[h], NN)).astype(BF16)
    for i in range(half):
        value_out[i] = value[heads_ref[own_at(i)]]
    pass_mid.start()
    for copy in get_wide:
        copy.wait()

    together = TOGETHER
    groups = per // together
    part_rows = rows // 2
    span = together * part_rows
    log2e = factor * math.log2(math.e)
    total_q[...] = jnp.zeros_like(total_q)
    total_v[...] = jnp.zeros_like(total_v)
    hand_out[...] = jnp.zeros_like(hand_out)
    lead = half - 1
    early = early_columns(kv, wide, group)
    narrow = early + (2 * wide + kv * HEAD_SIZE)
    if 2 * lead * wide < early:
        part_e[:, 2 * lead * wide : early] = jnp.zeros((rank, early - 2 * lead * wide), BF16)
    if narrow < part_e.shape[1]:
        part_e[:, narrow:] = jnp.zeros((rank, part_e.shape[1] - narrow), BF16)

    def slot_of(with_prior, i):
        side = parity if with_prior else 1 - parity
        last = i // lead
        return (1 - last) * (side * lead + i) * wide + last * (early + side * wide)

    def piled(array):
        return stack([array[:, k * HEAD_SIZE : (k + 1) * HEAD_SIZE] for k in range(together)])

    def phase(with_prior, start, stop):
        before = rows if with_prior else 0
        reaches = [before + part_rows, before + rows]
        place_of = prior_at if with_prior else own_at

        def opened(i, p, a, now):
            head = now["head"]
            at = slice(a * part_rows, (a + 1) * part_rows)
            cols = slice(p * together * HEAD_SIZE, (p + 1) * together * HEAD_SIZE)
            reach = reaches[a]
            adapted = dot(query_mid[at, :], qup[head, :, cols], NN)
            query = (fq[head, at, cols].astype(F32) + adapted).astype(BF16)
            scores = dot(now["keys"][:reach], piled(query), NT)
            return scores, dot(now["values"][:reach], piled(grad[head, at, cols]), NT)

        def weighed(a, scores, dprob):
            key_pos = lax.broadcasted_iota(jnp.int32, (part_rows, span), 0)
            query_pos = lax.broadcasted_iota(jnp.int32, (part_rows, span), 1)
            causal = key_pos <= lax.rem(query_pos, part_rows)
            free = reaches[a] - part_rows
            diagonal = jnp.where(causal, scores[free:], -jnp.inf)
            scores = stack([scores[:free], diagonal]) if free else diagonal
            top = jnp.max(scores, axis=0, keepdims=True)
            exponent = jnp.exp2((scores - top) * log2e)
            probs = exponent * (1.0 / jnp.sum(exponent, axis=0, keepdims=True))
            weights = probs.astype(BF16)
            delta = jnp.sum(probs * dprob, axis=0, keepdims=True)
            return weights, (probs * (dprob - delta)).astype(BF16)

        def closed(i, p, a, weights, dscore, now):
            pos, head = now["pos"], now["head"]
            cols = slice(p * together * HEAD_SIZE, (p + 1) * together * HEAD_SIZE)
            at = slice(a * part_rows, (a + 1) * part_rows)
            now["term", a] = dot(weights, piled(grad[head, at, cols]), NN)
            now["dq", a] = dot(now["keys_t"][:, : reaches[a]], dscore, NN).astype(BF16)
            if a == 0:
                return
            short, full = now["term", 0], now["term", 1]
            dv = stack([full[: reaches[0]] + short, full[reaches[0] :]])
            if p:
                dv = dv + now["dv"]
            now["dv"] = dv
            dquery = stack(
                [
                    beside(
                        [now["dq", b][:, k * part_rows : (k + 1) * part_rows] for b in range(2)]
                    )
                    for k in range(together)
                ]
            )
            at = slot_of(with_prior, i) + p * together * HEAD_SIZE
            at = pl.multiple_of(at, HEAD_SIZE)
            part_e[:, pl.ds(at, together * HEAD_SIZE)] = (
                dot(query_mid_t[...], dquery, NT) * factor
            ).astype(BF16)
            total_q[...] += dot(qup[head, :, cols], dquery, NN)
            if p < groups - 1:
                return
            up = vup[head]
            mine = dv[before:].astype(BF16)
            raw = dot(mid_out[...], mine, NN)
            total_v[...] += dot(up, mine, NT)
            if before:
                others = dv[:before].astype(BF16)
                raw = raw + dot(mid_in[...], others, NN)
                hand_out[...] += dot(up, others, NT)
            at = pl.multiple_of(early + 2 * wide + pos * HEAD_SIZE, HEAD_SIZE)
            part_e[:, pl.ds(at, HEAD_SIZE)] = raw.astype(BF16)

        def arrived(i):
            key_copy(i).wait_recv()
            value_copy(i).wait_recv()

        def body(i, carry):
            if with_prior:
                arrived(i)
            elif start == 0:
                value_copy(i).start()
            pos = place_of(i)
            head = heads_ref[pos]
            keys, values = key[head], value[head]
            if with_prior:
                keys, values = stack([key_in[i], keys]), stack([value_in[i], values])
            now = {"pos": pos, "head": head, "keys": keys, "values": values, "keys_t": keys.T}
            steps = [(p, a) for p in range(groups) for a in range(2)]
            begun, done = {}, {}
            for t in range(len(steps) + 2):
                if t < len(steps):
                    begun[t] = opened(i, *steps[t], now)
                if 0 <= t - 1 < len(steps):
                    done[t - 1] = weighed(steps[t - 1][1], *begun.pop(t - 1))
                if t >= 2:
                    closed(i, *steps[t - 2], *done.pop(t - 2), now)
            return carry

        if with_prior:
            pass_mid.wait_recv()
        lax.fori_loop(start, stop, body, 0)

    phase(False, 0, half - 1)
    key_copy(half - 1).start()
    value_copy(half - 1).start()
    phase(True, 0, half)

    late = part_e.shape[1] - early
    each = width // PIECES
    sums = [(part_e, full_e, 0, early), (part_e, full_e, early, late)]
    sums += [(part_s, full_s, c * each, each) for c in range(PIECES)]
    steps = 2 * (group - 1) + planes - 1
    sent = [[[], [], []] for _ in sums]

    def share(array, at, size, index):
        piece = size // group
        return array.at[:, pl.ds(pl.multiple_of(at + index * piece, LANES), piece)]

    def scatter(c):
        source, _, start, size = sums[c]
        for k in range(1, group):
            peer, device = in_group(k)
            at = c * steps + k - 1
            sent[c][0].append(
                remote(
                    share(source, start, size, peer),
                    parts[c].at[k - 1],
                    sem_send.at[at],
                    sem_recv.at[at],
                    device,
                )
            )

    def across(c):
        source, _, start, size = sums[c]
        column = columns[c]
        amount = share(source, start, size, me)[...].astype(F32)
        for k in range(1, group):
            sent[c][0][k - 1].wait_recv()
            amount = amount + parts[c][k - 1].astype(F32)
        column[plane] = amount.astype(BF16)
        for k in range(1, planes):
            at = c * steps + group - 1 + k - 1
            sent[c][1].append(
                remote(
                    column.at[plane],
                    column.at[plane],
                    sem_send.at[at],
                    sem_recv.at[at],
                    in_column(k),
                )
            )

    def gather(c):
        _, full, start, size = sums[c]
        for copy in sent[c][1]:
            copy.wait_recv()
        amount = columns[c][0].astype(F32)
        for i in range(1, planes):
            amount = amount + columns[c][i].astype(F32)
        share(full, start, size, me)[...] = amount.astype(BF16)
        for k in range(1, group):
            at = c * steps + group + planes - 2 + k - 1
            sent[c][2].append(
                remote(
                    share(full, start, size, me),
                    share(full, start, size, me),
                    sem_send.at[at],
                    sem_recv.at[at],
                    in_group(k)[1],
                )
            )

    pass_hand.start()
    scatter(0)
    phase(False, half - 1, half)
    scatter(1)
    pass_hand.wait_recv()
    inner = stack([total_q[...] * factor, total_v[...] + hand_in[...]]) * ADAPTER_SCALE
    inner = stack(split(inner.astype(BF16).astype(F32) * inverse_row))
    for c in range(PIECES):
        cols = slice(c * each, (c + 1) * each)
        out = dot(inner, x[:, cols], NN)
        part_s[:, cols] = (out[: 2 * rank] + out[2 * rank :]).astype(BF16)
        scatter(2 + c)
    for c in range(4):
        across(c)
    for c in range(4):
        gather(c)
    for i in range(half):
        key_copy(i).wait_send()
        value_copy(i).wait_send()
    pass_mid.wait_send()
    pass_hand.wait_send()
    for stage in range(3):
        for group_sent in sent:
            for copy in group_sent[stage]:
                copy.wait_send()
    for group_sent in sent:
        for copy in group_sent[2]:
            copy.wait_recv()


def fused(heads, x, fq, grads, keys, values, scale, qdown, vdown, qup, vup, seqs, planes):
    rows, width = x.shape
    rank = qdown.shape[0]
    half = heads.shape[0] // 2
    group = seqs * CORES
    kv = heads.shape[0]
    wide = fq.shape[1] // kv
    unit = group * LANES
    early = early_columns(kv, wide, group)
    late = -(-(2 * wide + keys.shape[1]) // unit) * unit
    operands = (x, fq, grads, keys, values, scale, qdown, vdown, qup, vup)
    vmem = pl.BlockSpec(memory_space=pltpu.VMEM)
    dma = pltpu.SemaphoreType.DMA
    sizes = ((rank, early + late), (2 * rank, width))
    cuts = ((rank, early), (rank, late)) + ((2 * rank, width // PIECES),) * PIECES
    passes = 2 * half + 2
    steps = len(cuts) * (2 * (group - 1) + planes - 1)
    blocks = lambda count: pltpu.VMEM((count, rows, HEAD_SIZE), BF16)
    def held(a):
        if a.shape[1] == width or a.shape[1] == LANES:
            return pltpu.VMEM(a.shape, a.dtype)
        return pltpu.VMEM((kv, a.shape[0], a.shape[1] // kv), a.dtype)

    return pl.pallas_call(
        functools.partial(fused_kernel, seqs, planes),
        in_specs=[pl.BlockSpec(memory_space=pltpu.HBM)] * (1 + len(operands)),
        out_specs=[vmem] * 2,
        out_shape=[jax.ShapeDtypeStruct(n, BF16) for n in sizes],
        scratch_shapes=[held(a) for a in operands]
        + [held(values)]
        + [blocks(half), blocks(half), pltpu.VMEM((rank, rows), BF16)] * 2
        + [pltpu.VMEM((rank, rows), F32)] * 2
        + [pltpu.VMEM(n, BF16) for n in sizes]
        + [tuple(pltpu.VMEM((group - 1, r, n // group), BF16) for r, n in cuts)]
        + [tuple(pltpu.VMEM((planes, r, n // group), BF16) for r, n in cuts)]
        + [dma((5 + 6 * kv + CHUNKS,)), dma((passes,)), dma((passes,))]
        + [dma((steps,)), dma((steps,))]
        + [pltpu.VMEM((rows, rank), BF16), pltpu.VMEM((rank, rows), BF16)]
        + [pltpu.VMEM((rank, rows), F32)] * 2
        + [pltpu.SMEM((kv,), jnp.int32)],
        compiler_params=pltpu.CompilerParams(
            collective_id=0,
            has_side_effects=True,
        ),
        name="fused",
    )(heads, *operands)


def finish_kernel(
    limit,
    early,
    heads_ref,
    full_e,
    full_s,
    scale_ref,
    qdown_ref,
    vdown_ref,
    qa_ref,
    qb_ref,
    va_ref,
    vb_ref,
    gain_ref,
):
    rank, width = qa_ref.shape
    kv = vb_ref.shape[1] // HEAD_SIZE
    wide = qb_ref.shape[1] // kv
    lead = kv // 2 - 1
    starts = []
    for pos in range(kv):
        side, i = pos // (lead + 1), pos % (lead + 1)
        starts.append(early + side * wide if i == lead else (side * lead + i) * wide)
    behind = early + 2 * wide
    squares = jnp.zeros((rank, LANES), F32)
    tops = jnp.zeros((1, LANES), F32)
    for i in range(width // LANES):
        cols = slice(i * LANES, (i + 1) * LANES)
        scale = scale_ref[i : i + 1, :].astype(F32)
        both = full_s[:, cols].astype(F32)
        query, value = both[:rank], both[rank:]
        gain = qdown_ref[:, cols].astype(F32) * query + vdown_ref[:, cols].astype(F32) * value
        gain = jnp.sum(gain, axis=0, keepdims=True)
        query, value = query * scale, value * scale
        squares = squares + query * query + value * value
        tops = tops + gain * gain
        qa_ref[:, cols], va_ref[:, cols] = query, value
        gain_ref[i : i + 1, :] = gain
    spans = [(start, wide) for start in starts] + [(behind, vb_ref.shape[1])]
    for start, size in spans:
        for i in range(size // LANES):
            piece = full_e[:, start + i * LANES : start + (i + 1) * LANES].astype(F32)
            squares = squares + piece * piece
    squares = jnp.sum(squares, axis=0, keepdims=True) + tops
    squares = jnp.sum(squares, axis=1, keepdims=True)
    scale = jnp.minimum(1.0, limit / jnp.sqrt(squares))
    qa_ref[...] = qa_ref[...] * scale
    va_ref[...] = va_ref[...] * scale
    gain_ref[...] = gain_ref[...] * scale
    for pos in range(kv):
        head = heads_ref[pos]
        at = pl.multiple_of(head * wide, HEAD_SIZE)
        qb_ref[:, pl.ds(at, wide)] = full_e[:, starts[pos] : starts[pos] + wide].astype(F32) * scale
        at = pl.multiple_of(head * HEAD_SIZE, HEAD_SIZE)
        first = behind + pos * HEAD_SIZE
        piece = full_e[:, first : first + HEAD_SIZE].astype(F32)
        vb_ref[:, pl.ds(at, HEAD_SIZE)] = piece * scale


def finished(heads, fulls, scale, qdown, vdown, limit, early, widths):
    rank, width = qdown.shape
    vmem = pl.BlockSpec(memory_space=pltpu.VMEM)
    return pl.pallas_call(
        functools.partial(finish_kernel, limit, early),
        in_specs=[pl.BlockSpec(memory_space=pltpu.SMEM)] + [vmem] * 5,
        out_specs=[vmem] * (len(widths) + 1),
        out_shape=[jax.ShapeDtypeStruct((rank, w), F32) for w in widths]
        + [jax.ShapeDtypeStruct((width // LANES, LANES), F32)],

        name="finished",
    )(heads, *fulls, scale, qdown, vdown)


def shards(
    layer_input,
    frozen_queries,
    frozen_keys,
    frozen_values,
    output_gradient,
    norm_scale_vector,
    query_down_weight,
    query_up_weight,
    value_down_weight,
    value_up_weight,
    head_ordering,
):
    seqs = lax.axis_size("seq")
    planes = lax.axis_size("dp") // CORES
    rank, width = query_down_weight.shape
    queries = query_up_weight.shape[1]
    kv = value_up_weight.shape[1]
    scale = norm_scale_vector.reshape(width // LANES, LANES)
    fulls = fused(
        head_ordering,
        layer_input[0],
        frozen_queries[0],
        output_gradient[0],
        frozen_keys[0],
        frozen_values[0],
        scale,
        query_down_weight,
        value_down_weight,
        query_up_weight,
        value_up_weight,
        seqs,
        planes,
    )
    limit = math.sqrt(rank * (2 * width + queries + kv) + width)
    qa, qb, va, vb, gain = finished(
        head_ordering,
        fulls,
        scale,
        query_down_weight,
        value_down_weight,
        limit,
        early_columns(head_ordering.shape[0], queries // head_ordering.shape[0], seqs * CORES),
        (width, queries, width, kv),
    )
    return (qa, qb, va, vb, gain.reshape(width))


def solution(mesh):
    placed = (
        P("dp", "seq", None),
        P("dp", "seq", None),
        P("dp", "seq", None),
        P("dp", "seq", None),
        P("dp", "seq", None),
        P(),
        P(),
        P(),
        P(),
        P(),
        P(),
    )
    return jax.shard_map(
        shards, mesh=mesh, in_specs=placed, out_specs=(P(), P(), P(), P(), P()), check_vma=False
    )
```

```python
import functools
import math

import jax
import jax.numpy as jnp
from jax import lax
from jax.experimental import pallas as pl
from jax.experimental.pallas import tpu as pltpu
from jax.sharding import PartitionSpec as P

HEAD_SIZE = 128
CORES = 2
LANES = 128
TOGETHER = 8
CHUNKS = 4
PIECES = 2

EPS = 1e-05
ADAPTER_SCALE = 2.0
F32 = jnp.float32
BF16 = jnp.bfloat16
NT = (((1,), (1,)), ((), ()))
NN = (((1,), (0,)), ((), ()))
MESH = pl.DeviceIdType.MESH


def dot(left, right, dims):
    return lax.dot_general(left, right, dims, preferred_element_type=F32)


def stack(pieces):
    return jnp.concatenate(pieces, axis=0)


def beside(pieces):
    return jnp.concatenate(pieces, axis=1)


def split(value):
    high = value.astype(BF16)
    return high, (value - high.astype(F32)).astype(BF16)


def early_columns(kv, wide, group):
    unit = group * LANES
    return -(-2 * (kv // 2 - 1) * wide // unit) * unit


def fused_kernel(
    seqs,
    planes,
    heads_hbm,
    x_hbm,
    fq_hbm,
    grad_hbm,
    key_hbm,
    fv_hbm,
    scale_hbm,
    qdown_hbm,
    vdown_hbm,
    qup_hbm,
    vup_hbm,
    full_e,
    full_s,
    x,
    fq,
    grad,
    key,
    fv,
    scale,
    qdown,
    vdown,
    qup,
    vup,
    value,
    key_out,
    value_out,
    mid_out,
    key_in,
    value_in,
    mid_in,
    hand_out,
    hand_in,
    part_e,
    part_s,
    parts,
    columns,
    sem_load,
    sem_pass_send,
    sem_pass_recv,
    sem_send,
    sem_recv,
    query_mid,
    query_mid_t,
    total_q,
    total_v,
    heads_ref,
):
    rows, width = x.shape
    rank = qdown.shape[0]
    kv, _, wide = fq.shape
    half = kv // 2
    per = wide // HEAD_SIZE
    queries = kv * wide
    factor = 1.0 / math.sqrt(HEAD_SIZE)
    group = seqs * CORES
    seq = lax.axis_index("seq")
    place = lax.axis_index("dp")
    plane = place // CORES
    me = seq * CORES + place % CORES
    parity = lax.rem(seq, 2)
    following = {"seq": lax.rem(seq + 1, seqs)}
    previous = {"seq": lax.rem(seq + seqs - 1, seqs)}

    def in_group(k):
        peer = lax.rem(me + k, group)
        return peer, {"seq": peer // CORES, "dp": plane * CORES + peer % CORES}

    def in_column(k):
        return {"dp": lax.rem(plane + k, planes) * CORES + place % CORES}

    loads = []

    def load(source, target):
        copy = pltpu.make_async_copy(source, target, sem_load.at[len(loads)])
        copy.start()
        loads.append(copy)
        return copy

    def by_head(source, target):
        size = target.shape[2]
        return [load(source.at[:, h * size : (h + 1) * size], target.at[h]) for h in range(kv)]

    block = width // CHUNKS
    get_key = [load(heads_hbm, heads_ref)] + by_head(key_hbm, key)
    get_small = [
        load(s, t) for s, t in ((scale_hbm, scale), (qdown_hbm, qdown), (vdown_hbm, vdown))
    ]
    get_x = [
        load(x_hbm.at[:, c * block : (c + 1) * block], x.at[:, c * block : (c + 1) * block])
        for c in range(CHUNKS)
    ]
    get_value = by_head(fv_hbm, fv) + by_head(vup_hbm, vup) + by_head(qup_hbm, qup)
    get_wide = by_head(fq_hbm, fq) + by_head(grad_hbm, grad)

    barrier = pltpu.get_barrier_semaphore()
    for k in range(1, group):
        pl.semaphore_signal(barrier, inc=1, device_id=in_group(k)[1], device_id_type=MESH)
    for k in range(1, planes):
        pl.semaphore_signal(barrier, inc=1, device_id=in_column(k), device_id_type=MESH)

    def remote(source, target, send, recv, device):
        copy = pltpu.make_async_remote_copy(
            src_ref=source,
            dst_ref=target,
            send_sem=send,
            recv_sem=recv,
            device_id=device,
            device_id_type=MESH,
        )
        copy.start()
        return copy

    def handing(source, target, device, at):
        return pltpu.make_async_remote_copy(
            src_ref=source,
            dst_ref=target,
            send_sem=sem_pass_send.at[at],
            recv_sem=sem_pass_recv.at[at],
            device_id=device,
            device_id_type=MESH,
        )

    key_copy = lambda i: handing(key_out.at[i], key_in.at[i], following, i)
    value_copy = lambda i: handing(value_out.at[i], value_in.at[i], following, half + i)
    pass_mid = handing(mid_out, mid_in, following, 2 * half)
    pass_hand = handing(hand_out, hand_in, previous, 2 * half + 1)

    own_at = lambda i: (1 - parity) * half + i
    prior_at = lambda i: parity * half + i

    for copy in get_key:
        copy.wait()
    for i in range(half):
        key_out[i] = key[heads_ref[own_at(i)]]
    for copy in get_small:
        copy.wait()
    squares = jnp.zeros((rows, LANES), F32)
    each = block // LANES
    for c in range(CHUNKS):
        get_x[c].wait()
        for b in range(c * each, (c + 1) * each):
            part = x[:, b * LANES : (b + 1) * LANES].astype(F32)
            squares = squares + part * part
        if c == 0:
            pl.semaphore_wait(barrier, group + planes - 2)
            for i in range(half - 1):
                key_copy(i).start()
    inverse = lax.rsqrt(jnp.sum(squares, axis=1, keepdims=True) * (1.0 / width) + EPS)
    inverse_row = jnp.broadcast_to(inverse, (rows, LANES)).T[: 2 * rank]
    mids = [jnp.zeros((rows // 2, 2 * rank), F32)] * 2
    for c in range(CHUNKS):
        cols = slice(c * block, (c + 1) * block)
        down = stack([qdown[:, cols], vdown[:, cols]])
        for r in range(2):
            at = slice(r * rows // 2, (r + 1) * rows // 2)
            normed = []
            for b in range(c * each, (c + 1) * each):
                unit = x[at, b * LANES : (b + 1) * LANES].astype(F32) * inverse[at]
                normed.append((unit * scale[b : b + 1, :].astype(F32)).astype(BF16))
            mids[r] = mids[r] + dot(beside(normed), down, NT)
    mids = stack(mids).astype(BF16)
    twice = (mids * ADAPTER_SCALE).astype(BF16)
    query_mid[...] = twice[:, :rank]
    value_mid = twice[:, rank:]
    eye_r = lax.broadcasted_iota(jnp.int32, (2 * rank, 2 * rank), 0)
    eye_c = lax.broadcasted_iota(jnp.int32, (2 * rank, 2 * rank), 1)
    eye = jnp.where(eye_r == eye_c, ADAPTER_SCALE, 0.0).astype(BF16)
    mids_t = dot(eye, mids, NT)
    query_mid_t[...] = mids_t[:rank].astype(BF16)
    mid_out[...] = mids_t[rank:].astype(BF16)
    for copy in get_value:
        copy.wait()
    for h in range(kv):
        value[h] = (fv[h].astype(F32) + dot(value_mid, vup[h], NN)).astype(BF16)
    for i in range(half):
        value_out[i] = value[heads_ref[own_at(i)]]
    pass_mid.start()
    value_copy(0).start()
    for copy in get_wide:
        copy.wait()

    together = TOGETHER
    groups = per // together
    part_rows = rows // 2
    span = together * part_rows
    log2e = factor * math.log2(math.e)
    total_q[...] = jnp.zeros_like(total_q)
    total_v[...] = jnp.zeros_like(total_v)
    hand_out[...] = jnp.zeros_like(hand_out)
    lead = half - 1
    early = early_columns(kv, wide, group)
    narrow = early + (2 * wide + kv * HEAD_SIZE)
    if 2 * lead * wide < early:
        part_e[:, 2 * lead * wide : early] = jnp.zeros((rank, early - 2 * lead * wide), BF16)
    if narrow < part_e.shape[1]:
        part_e[:, narrow:] = jnp.zeros((rank, part_e.shape[1] - narrow), BF16)

    def slot_of(with_prior, i):
        side = parity if with_prior else 1 - parity
        last = i // lead
        return (1 - last) * (side * lead + i) * wide + last * (early + side * wide)

    def piled(array):
        return stack([array[:, k * HEAD_SIZE : (k + 1) * HEAD_SIZE] for k in range(together)])

    def phase(with_prior, start, stop):
        before = rows if with_prior else 0
        reaches = [before + part_rows, before + rows]
        place_of = prior_at if with_prior else own_at

        def opened(i, p, a, now):
            head = now["head"]
            at = slice(a * part_rows, (a + 1) * part_rows)
            cols = slice(p * together * HEAD_SIZE, (p + 1) * together * HEAD_SIZE)
            reach = reaches[a]
            adapted = dot(query_mid[at, :], qup[head, :, cols], NN)
            query = (fq[head, at, cols].astype(F32) + adapted).astype(BF16)
            scores = dot(now["keys"][:reach], piled(query), NT)
            return scores, dot(now["values"][:reach], piled(grad[head, at, cols]), NT)

        def weighed(a, scores, dprob):
            key_pos = lax.broadcasted_iota(jnp.int32, (part_rows, span), 0)
            query_pos = lax.broadcasted_iota(jnp.int32, (part_rows, span), 1)
            causal = key_pos <= lax.rem(query_pos, part_rows)
            free = reaches[a] - part_rows
            diagonal = jnp.where(causal, scores[free:], -jnp.inf)
            scores = stack([scores[:free], diagonal]) if free else diagonal
            top = jnp.max(scores, axis=0, keepdims=True)
            exponent = jnp.exp2((scores - top) * log2e)
            probs = exponent * (1.0 / jnp.sum(exponent, axis=0, keepdims=True))
            weights = probs.astype(BF16)
            delta = jnp.sum(probs * dprob, axis=0, keepdims=True)
            return weights, (probs * (dprob - delta)).astype(BF16)

        def closed(i, p, a, weights, dscore, now):
            pos, head = now["pos"], now["head"]
            cols = slice(p * together * HEAD_SIZE, (p + 1) * together * HEAD_SIZE)
            at = slice(a * part_rows, (a + 1) * part_rows)
            now["term", a] = dot(weights, piled(grad[head, at, cols]), NN)
            now["dq", a] = dot(now["keys_t"][:, : reaches[a]], dscore, NN).astype(BF16)
            if a == 0:
                return
            short, full = now["term", 0], now["term", 1]
            dv = stack([full[: reaches[0]] + short, full[reaches[0] :]])
            if p:
                dv = dv + now["dv"]
            now["dv"] = dv
            dquery = stack(
                [
                    beside(
                        [now["dq", b][:, k * part_rows : (k + 1) * part_rows] for b in range(2)]
                    )
                    for k in range(together)
                ]
            )
            at = slot_of(with_prior, i) + p * together * HEAD_SIZE
            at = pl.multiple_of(at, HEAD_SIZE)
            part_e[:, pl.ds(at, together * HEAD_SIZE)] = (
                dot(query_mid_t[...], dquery, NT) * factor
            ).astype(BF16)
            total_q[...] += dot(qup[head, :, cols], dquery, NN)
            if p < groups - 1:
                return
            up = vup[head]
            mine = dv[before:].astype(BF16)
            raw = dot(mid_out[...], mine, NN)
            total_v[...] += dot(up, mine, NT)
            if before:
                others = dv[:before].astype(BF16)
                raw = raw + dot(mid_in[...], others, NN)
                hand_out[...] += dot(up, others, NT)
            at = pl.multiple_of(early + 2 * wide + pos * HEAD_SIZE, HEAD_SIZE)
            part_e[:, pl.ds(at, HEAD_SIZE)] = raw.astype(BF16)

        def arrived(i):
            key_copy(i).wait_recv()
            value_copy(i).wait_recv()

        def body(i, carry):
            if with_prior:
                arrived(i)
            elif start == 0:
                value_copy(i + 1).start()
            pos = place_of(i)
            head = heads_ref[pos]
            keys, values = key[head], value[head]
            if with_prior:
                keys, values = stack([key_in[i], keys]), stack([value_in[i], values])
            now = {"pos": pos, "head": head, "keys": keys, "values": values, "keys_t": keys.T}
            steps = [(p, a) for p in range(groups) for a in range(2)]
            begun, done = {}, {}
            for t in range(len(steps) + 2):
                if t < len(steps):
                    begun[t] = opened(i, *steps[t], now)
                if 0 <= t - 1 < len(steps):
                    done[t - 1] = weighed(steps[t - 1][1], *begun.pop(t - 1))
                if t >= 2:
                    closed(i, *steps[t - 2], *done.pop(t - 2), now)
            return carry

        if with_prior:
            pass_mid.wait_recv()
        lax.fori_loop(start, stop, body, 0)

    phase(False, 0, half - 1)
    key_copy(half - 1).start()
    phase(True, 0, half)

    late = part_e.shape[1] - early
    each = width // PIECES
    sums = [(part_e, full_e, 0, early), (part_e, full_e, early, late)]
    sums += [(part_s, full_s, c * each, each) for c in range(PIECES)]
    steps = 2 * (group - 1) + planes - 1
    sent = [[[], [], []] for _ in sums]

    def share(array, at, size, index):
        piece = size // group
        return array.at[:, pl.ds(pl.multiple_of(at + index * piece, LANES), piece)]

    def scatter(c):
        source, _, start, size = sums[c]
        for k in range(1, group):
            peer, device = in_group(k)
            at = c * steps + k - 1
            sent[c][0].append(
                remote(
                    share(source, start, size, peer),
                    parts[c].at[k - 1],
                    sem_send.at[at],
                    sem_recv.at[at],
                    device,
                )
            )

    def across(c):
        source, _, start, size = sums[c]
        column = columns[c]
        amount = share(source, start, size, me)[...].astype(F32)
        for k in range(1, group):
            sent[c][0][k - 1].wait_recv()
            amount = amount + parts[c][k - 1].astype(F32)
        column[plane] = amount.astype(BF16)
        for k in range(1, planes):
            at = c * steps + group - 1 + k - 1
            sent[c][1].append(
                remote(
                    column.at[plane],
                    column.at[plane],
                    sem_send.at[at],
                    sem_recv.at[at],
                    in_column(k),
                )
            )

    def gather(c):
        _, full, start, size = sums[c]
        for copy in sent[c][1]:
            copy.wait_recv()
        amount = columns[c][0].astype(F32)
        for i in range(1, planes):
            amount = amount + columns[c][i].astype(F32)
        share(full, start, size, me)[...] = amount.astype(BF16)
        for k in range(1, group):
            at = c * steps + group + planes - 2 + k - 1
            sent[c][2].append(
                remote(
                    share(full, start, size, me),
                    share(full, start, size, me),
                    sem_send.at[at],
                    sem_recv.at[at],
                    in_group(k)[1],
                )
            )

    pass_hand.start()
    scatter(0)
    phase(False, half - 1, half)
    scatter(1)
    pass_hand.wait_recv()
    inner = stack([total_q[...] * factor, total_v[...] + hand_in[...]]) * ADAPTER_SCALE
    inner = stack(split(inner.astype(BF16).astype(F32) * inverse_row))
    for c in range(PIECES):
        cols = slice(c * each, (c + 1) * each)
        out = dot(inner, x[:, cols], NN)
        part_s[:, cols] = (out[: 2 * rank] + out[2 * rank :]).astype(BF16)
        scatter(2 + c)
    for c in range(4):
        across(c)
    for c in range(4):
        gather(c)
    for i in range(half):
        key_copy(i).wait_send()
        value_copy(i).wait_send()
    pass_mid.wait_send()
    pass_hand.wait_send()
    for stage in range(3):
        for group_sent in sent:
            for copy in group_sent[stage]:
                copy.wait_send()
    for group_sent in sent:
        for copy in group_sent[2]:
            copy.wait_recv()


def fused(heads, x, fq, grads, keys, values, scale, qdown, vdown, qup, vup, seqs, planes):
    rows, width = x.shape
    rank = qdown.shape[0]
    half = heads.shape[0] // 2
    group = seqs * CORES
    kv = heads.shape[0]
    wide = fq.shape[1] // kv
    unit = group * LANES
    early = early_columns(kv, wide, group)
    late = -(-(2 * wide + keys.shape[1]) // unit) * unit
    operands = (x, fq, grads, keys, values, scale, qdown, vdown, qup, vup)
    vmem = pl.BlockSpec(memory_space=pltpu.VMEM)
    dma = pltpu.SemaphoreType.DMA
    sizes = ((rank, early + late), (2 * rank, width))
    cuts = ((rank, early), (rank, late)) + ((2 * rank, width // PIECES),) * PIECES
    passes = 2 * half + 2
    steps = len(cuts) * (2 * (group - 1) + planes - 1)
    blocks = lambda count: pltpu.VMEM((count, rows, HEAD_SIZE), BF16)
    def held(a):
        if a.shape[1] == width or a.shape[1] == LANES:
            return pltpu.VMEM(a.shape, a.dtype)
        return pltpu.VMEM((kv, a.shape[0], a.shape[1] // kv), a.dtype)

    return pl.pallas_call(
        functools.partial(fused_kernel, seqs, planes),
        in_specs=[pl.BlockSpec(memory_space=pltpu.HBM)] * (1 + len(operands)),
        out_specs=[vmem] * 2,
        out_shape=[jax.ShapeDtypeStruct(n, BF16) for n in sizes],
        scratch_shapes=[held(a) for a in operands]
        + [held(values)]
        + [blocks(half), blocks(half), pltpu.VMEM((rank, rows), BF16)] * 2
        + [pltpu.VMEM((rank, rows), F32)] * 2
        + [pltpu.VMEM(n, BF16) for n in sizes]
        + [tuple(pltpu.VMEM((group - 1, r, n // group), BF16) for r, n in cuts)]
        + [tuple(pltpu.VMEM((planes, r, n // group), BF16) for r, n in cuts)]
        + [dma((5 + 6 * kv + CHUNKS,)), dma((passes,)), dma((passes,))]
        + [dma((steps,)), dma((steps,))]
        + [pltpu.VMEM((rows, rank), BF16), pltpu.VMEM((rank, rows), BF16)]
        + [pltpu.VMEM((rank, rows), F32)] * 2
        + [pltpu.SMEM((kv,), jnp.int32)],
        compiler_params=pltpu.CompilerParams(
            collective_id=0,
            has_side_effects=True,
        ),
        name="fused",
    )(heads, *operands)


def finish_kernel(
    limit,
    early,
    heads_ref,
    full_e,
    full_s,
    scale_ref,
    qdown_ref,
    vdown_ref,
    qa_ref,
    qb_ref,
    va_ref,
    vb_ref,
    gain_ref,
):
    rank, width = qa_ref.shape
    kv = vb_ref.shape[1] // HEAD_SIZE
    wide = qb_ref.shape[1] // kv
    lead = kv // 2 - 1
    starts = []
    for pos in range(kv):
        side, i = pos // (lead + 1), pos % (lead + 1)
        starts.append(early + side * wide if i == lead else (side * lead + i) * wide)
    behind = early + 2 * wide
    squares = jnp.zeros((rank, LANES), F32)
    tops = jnp.zeros((1, LANES), F32)
    for i in range(width // LANES):
        cols = slice(i * LANES, (i + 1) * LANES)
        scale = scale_ref[i : i + 1, :].astype(F32)
        both = full_s[:, cols].astype(F32)
        query, value = both[:rank], both[rank:]
        gain = qdown_ref[:, cols].astype(F32) * query + vdown_ref[:, cols].astype(F32) * value
        gain = jnp.sum(gain, axis=0, keepdims=True)
        query, value = query * scale, value * scale
        squares = squares + query * query + value * value
        tops = tops + gain * gain
        qa_ref[:, cols], va_ref[:, cols] = query, value
        gain_ref[i : i + 1, :] = gain
    spans = [(start, wide) for start in starts] + [(behind, vb_ref.shape[1])]
    for start, size in spans:
        for i in range(size // LANES):
            piece = full_e[:, start + i * LANES : start + (i + 1) * LANES].astype(F32)
            squares = squares + piece * piece
    squares = jnp.sum(squares, axis=0, keepdims=True) + tops
    squares = jnp.sum(squares, axis=1, keepdims=True)
    scale = jnp.minimum(1.0, limit / jnp.sqrt(squares))
    qa_ref[...] = qa_ref[...] * scale
    va_ref[...] = va_ref[...] * scale
    gain_ref[...] = gain_ref[...] * scale
    for pos in range(kv):
        head = heads_ref[pos]
        at = pl.multiple_of(head * wide, HEAD_SIZE)
        qb_ref[:, pl.ds(at, wide)] = full_e[:, starts[pos] : starts[pos] + wide].astype(F32) * scale
        at = pl.multiple_of(head * HEAD_SIZE, HEAD_SIZE)
        first = behind + pos * HEAD_SIZE
        piece = full_e[:, first : first + HEAD_SIZE].astype(F32)
        vb_ref[:, pl.ds(at, HEAD_SIZE)] = piece * scale


def finished(heads, fulls, scale, qdown, vdown, limit, early, widths):
    rank, width = qdown.shape
    vmem = pl.BlockSpec(memory_space=pltpu.VMEM)
    return pl.pallas_call(
        functools.partial(finish_kernel, limit, early),
        in_specs=[pl.BlockSpec(memory_space=pltpu.SMEM)] + [vmem] * 5,
        out_specs=[vmem] * (len(widths) + 1),
        out_shape=[jax.ShapeDtypeStruct((rank, w), F32) for w in widths]
        + [jax.ShapeDtypeStruct((width // LANES, LANES), F32)],

        name="finished",
    )(heads, *fulls, scale, qdown, vdown)


def shards(
    layer_input,
    frozen_queries,
    frozen_keys,
    frozen_values,
    output_gradient,
    norm_scale_vector,
    query_down_weight,
    query_up_weight,
    value_down_weight,
    value_up_weight,
    head_ordering,
):
    seqs = lax.axis_size("seq")
    planes = lax.axis_size("dp") // CORES
    rank, width = query_down_weight.shape
    queries = query_up_weight.shape[1]
    kv = value_up_weight.shape[1]
    scale = norm_scale_vector.reshape(width // LANES, LANES)
    fulls = fused(
        head_ordering,
        layer_input[0],
        frozen_queries[0],
        output_gradient[0],
        frozen_keys[0],
        frozen_values[0],
        scale,
        query_down_weight,
        value_down_weight,
        query_up_weight,
        value_up_weight,
        seqs,
        planes,
    )
    limit = math.sqrt(rank * (2 * width + queries + kv) + width)
    qa, qb, va, vb, gain = finished(
        head_ordering,
        fulls,
        scale,
        query_down_weight,
        value_down_weight,
        limit,
        early_columns(head_ordering.shape[0], queries // head_ordering.shape[0], seqs * CORES),
        (width, queries, width, kv),
    )
    return (qa, qb, va, vb, gain.reshape(width))


def solution(mesh):
    placed = (
        P("dp", "seq", None),
        P("dp", "seq", None),
        P("dp", "seq", None),
        P("dp", "seq", None),
        P("dp", "seq", None),
        P(),
        P(),
        P(),
        P(),
        P(),
        P(),
    )
    return jax.shard_map(
        shards, mesh=mesh, in_specs=placed, out_specs=(P(), P(), P(), P(), P()), check_vma=False
    )
```
